256 devices in a mesh: seqhi: 16 (over x, z_lo, core), seqlo: 16 (over z_hi, y).
Axes of the slice: x: 4, y: 4, z: 8 (z_hi: 4, z_lo: 2; z = z_hi * 2 + z_lo), core: 2. Of those that a mesh axis runs over, the one named last changes fastest.
Arguments:
- queries: bfloat16 [65536, 2048], P(('seqhi', 'seqlo')), may hold values from -6 to 6
- keys: bfloat16 [65536, 128], P(('seqhi', 'seqlo')), may hold values from -6 to 6
- values: bfloat16 [65536, 128], P(('seqhi', 'seqlo')), may hold values from -6 to 6
- outputs: bfloat16 [65536, 2048], P(('seqhi', 'seqlo')), may hold values from -6 to 6
- out_grad: bfloat16 [65536, 2048], P(('seqhi', 'seqlo')), may hold values from -96 to 96
- lse: float32 [16, 65536], P(None, ('seqhi', 'seqlo')), may hold values from 7 to 9
- sink_keys: bfloat16 [128, 128], replicated, may hold values from -6 to 6
- sink_values: bfloat16 [128, 128], replicated, may hold values from -6 to 6
- window_len: int32 [16], replicated, may hold values from 256 to 2048, as said below
- sink_live: int32 [16], replicated, may hold values from 32 to 128, as said below
Outputs:
- query_grad: float32 [65536, 2048], P(('seqhi', 'seqlo'))
- key_grad: float32 [65536, 128], P(('seqhi', 'seqlo'))
- value_grad: float32 [65536, 128], P(('seqhi', 'seqlo'))
- sink_key_grad: float32 [128, 128], replicated
- sink_value_grad: float32 [128, 128], replicated
The draws below stay inside these ranges and needn't reach their ends.
Inputs may be any that keep to these rules, and one draw needn't show every extreme that they name: `window_len`: one head's window is exactly 2048. `sink_live`: one head reads all 128 initial keys.
All inputs are finite; a program needn't handle non-finite values.
Results may differ from the reference program's by a relative error of at most 0.0039.
Values may be sent and summed in bfloat16 or wider, within the bound.
A program may use at most 64 MiB of HBM per device.

```python
import jax
import jax.numpy as jnp
from jax import lax

H = 16
DH = 128
WIN = 2048
SINK = 128
TOK_DEV = 256
TOKENS = 65536


def draw_window_len(key, part):
    key_spans, key_top = jax.random.split(jax.random.fold_in(key, 11))
    spans = jax.random.randint(key_spans, (H,), WIN // 8, WIN + 1, dtype=jnp.int32)
    chosen = jax.random.randint(key_top, (), 0, H, dtype=jnp.int32)
    return jnp.where(jnp.arange(H, dtype=jnp.int32) == chosen, WIN, spans).astype(jnp.int32)


def draw_sink_live(key, part):
    key_spans, key_top = jax.random.split(jax.random.fold_in(key, 23))
    spans = jax.random.randint(key_spans, (H,), SINK // 4, SINK + 1, dtype=jnp.int32)
    chosen = jax.random.randint(key_top, (), 0, H, dtype=jnp.int32)
    return jnp.where(jnp.arange(H, dtype=jnp.int32) == chosen, SINK, spans).astype(jnp.int32)


def level_of(stream_key, dims, shards, least, largest):
    level, own = 1.0, jax.random.fold_in(stream_key, 6)
    for axis_at, parts in shards:
        draws = jnp.exp(jax.random.uniform(jax.random.fold_in(own, axis_at), (parts,), jnp.float32, least / len(shards), largest / len(shards)))
        level = level * jnp.repeat(draws, dims[axis_at] // parts).reshape([-1 if axis == axis_at else 1 for axis in range(len(dims))])
    return level


def gaussian(key, shape, deviation, limit, cuts=(), kind=jnp.bfloat16):
    values = jax.random.normal(key, shape, jnp.float32) * deviation
    if len(cuts) > 0:
        values = level_of(key, shape, cuts, -0.22, 0.18) * values
    return jnp.clip(values, min=-limit, max=limit).astype(kind)


def setup_inputs(seed: int = 0) -> dict:
    seeds = jax.random.split(jax.random.key(seed), 11)
    queries = gaussian(seeds[0], (TOKENS, H * DH), 1.0, 6.0, ((0, 256),))
    keys = gaussian(seeds[1], (TOKENS, DH), 1.0, 6.0, ((0, 256),))
    values = gaussian(seeds[2], (TOKENS, DH), 1.0, 6.0, ((0, 256),))
    outputs = gaussian(seeds[3], (TOKENS, H * DH), 1.0, 6.0, ((0, 256),))
    out_grad = gaussian(seeds[4], (TOKENS, H * DH), 16.0, 96.0, ((0, 256),))
    lse = jnp.clip(7.0 + 2.0 * jax.random.uniform(seeds[5], (H, TOKENS), jnp.float32) ** level_of(seeds[5], (H, TOKENS), ((1, 256),), -0.2, 0.2), 7.0, 9.0)
    sink_keys = gaussian(seeds[6], (SINK, DH), 1.0, 6.0)
    sink_values = gaussian(seeds[7], (SINK, DH), 1.0, 6.0)
    window_len = draw_window_len(jax.random.fold_in(seeds[10], 71), 0)
    sink_live = draw_sink_live(jax.random.fold_in(seeds[10], 71), 0)
    return dict(queries=queries, keys=keys, values=values, outputs=outputs, out_grad=out_grad, lse=lse, sink_keys=sink_keys, sink_values=sink_values, window_len=window_len, sink_live=sink_live)


def low_round(array_value):
    return lax.optimization_barrier(array_value.astype(jnp.bfloat16)).astype(jnp.float32)


def reference(queries, keys, values, outputs, out_grad, lse, sink_keys, sink_values, window_len, sink_live):
    reach_count = WIN // TOK_DEV
    block_count = TOKENS // TOK_DEV
    key_count = (reach_count + 1) * TOK_DEV
    score_scale = DH ** -0.5
    joined = jnp.concatenate([keys, values], axis=1)
    padded = jnp.concatenate([jnp.zeros((reach_count * TOK_DEV, 2 * DH), jnp.bfloat16), joined], axis=0)
    sink_key_f = sink_keys.astype(jnp.float32)
    sink_value_f = sink_values.astype(jnp.float32)
    key_index = jnp.arange(key_count, dtype=jnp.int32)
    query_index = reach_count * TOK_DEV + jnp.arange(TOK_DEV, dtype=jnp.int32)
    distance_grid = query_index[:, None] - key_index[None, :]
    sink_index = jnp.arange(SINK, dtype=jnp.int32)

    def one_block(state_pair, block_id):
        grad_store, sink_grad = state_pair
        begin = (block_id * TOK_DEV).astype(jnp.int32)
        query_block = lax.dynamic_slice_in_dim(queries, begin, TOK_DEV, 0).reshape(TOK_DEV, H, DH).astype(jnp.float32)
        out_block = lax.dynamic_slice_in_dim(outputs, begin, TOK_DEV, 0).reshape(TOK_DEV, H, DH).astype(jnp.float32)
        grad_block = lax.dynamic_slice_in_dim(out_grad, begin, TOK_DEV, 0).reshape(TOK_DEV, H, DH).astype(jnp.float32)
        lse_block = lax.dynamic_slice_in_dim(lse, begin, TOK_DEV, 1)
        key_value = lax.dynamic_slice_in_dim(padded, begin, key_count, 0).astype(jnp.float32)
        key_part = key_value[:, :DH]
        value_part = key_value[:, DH:]
        first_valid = ((reach_count - block_id) * TOK_DEV).astype(jnp.int32)
        inside = (distance_grid >= 0)[None] & (distance_grid[None] < window_len[:, None, None]) & (key_index >= first_valid)[None, None, :]
        scores = jnp.einsum("thd,kd->htk", query_block, key_part) * score_scale
        probabilities = jnp.where(inside, jnp.exp(scores - lse_block[:, :, None]), 0.0)
        row_delta = jnp.einsum("thd,thd->ht", grad_block, out_block)
        dprobs = jnp.einsum("thd,kd->htk", grad_block, value_part)
        dscores = probabilities * (dprobs - row_delta[:, :, None])
        sink_inside = sink_index[None, None, :] < sink_live[:, None, None]
        sink_scores = jnp.einsum("thd,sd->hts", query_block, sink_key_f) * score_scale
        sink_probs = jnp.where(sink_inside, jnp.exp(sink_scores - lse_block[:, :, None]), 0.0)
        sink_dprobs = jnp.einsum("thd,sd->hts", grad_block, sink_value_f)
        sink_dscores = sink_probs * (sink_dprobs - row_delta[:, :, None])
        probs_low = low_round(probabilities)
        dscores_low = low_round(dscores)
        sink_probs_low = low_round(sink_probs)
        sink_ds_low = low_round(sink_dscores)
        query_grad = (jnp.einsum("htk,kd->thd", dscores_low, key_part) + jnp.einsum("hts,sd->thd", sink_ds_low, sink_key_f)) * score_scale
        key_grad = jnp.einsum("htk,thd->kd", dscores_low, query_block) * score_scale
        value_grad = jnp.einsum("htk,thd->kd", probs_low, grad_block)
        sink_kgrad = jnp.einsum("hts,thd->sd", sink_ds_low, query_block) * score_scale
        sink_vgrad = jnp.einsum("hts,thd->sd", sink_probs_low, grad_block)
        current = lax.dynamic_slice_in_dim(grad_store, begin, key_count, 0)
        grad_store = lax.dynamic_update_slice_in_dim(grad_store, current + jnp.concatenate([key_grad, value_grad], axis=1), begin, 0)
        sink_grad = sink_grad + jnp.concatenate([sink_kgrad, sink_vgrad], axis=1)
        return (grad_store, sink_grad), query_grad.reshape(TOK_DEV, H * DH)

    start_state = (jnp.zeros((TOKENS + reach_count * TOK_DEV, 2 * DH), jnp.float32), jnp.zeros((SINK, 2 * DH), jnp.float32))
    (grad_store, sink_grad), query_grads = lax.scan(one_block, start_state, jnp.arange(block_count, dtype=jnp.int32))
    query_grad = query_grads.reshape(TOKENS, H * DH)
    pair_grad = grad_store[reach_count * TOK_DEV:]
    return query_grad, pair_grad[:, :DH], pair_grad[:, DH:], sink_grad[:, :DH], sink_grad[:, DH:]
```

```python
import functools
import math

import jax
import jax.numpy as jnp
from jax import lax
from jax.experimental import pallas as pl
from jax.experimental.pallas import tpu as pltpu
from jax.sharding import PartitionSpec as P

MESH = pl.DeviceIdType.MESH
F32 = jnp.float32
BF16 = jnp.bfloat16
HI = 16
LO = 16
NDEV = HI * LO
COLS = 4
REACH = 8
TOK = 256
DH = 128
HEADS = 16
SCALE = DH ** (-0.5)
EXP2_SCALE = SCALE * math.log2(math.e)


def place(device):
    device = (device + NDEV) % NDEV
    return (device // LO, device % LO)


def whoami():
    hi, lo = lax.axis_index("seqhi"), lax.axis_index("seqlo")
    return hi, lo, hi * LO + lo


def greet(targets):
    barrier = pltpu.get_barrier_semaphore()
    for target in targets:
        pl.semaphore_signal(barrier, inc=1, device_id=target, device_id_type=MESH)
    pl.semaphore_wait(barrier, len(targets))


def gather_kernel(keys, values, out, local_sem, send_sem, recv_sem):
    _, _, me = whoami()
    col = me % COLS
    mates = [me - col + (col + j) % COLS for j in range(1, COLS)]
    cols = [(col + j) % COLS for j in range(1, COLS)]
    greet([place(me + COLS), place(me - COLS)] + [place(m) for m in mates])

    load_k = pltpu.make_async_copy(keys, out.at[REACH, 0], local_sem.at[0])
    load_v = pltpu.make_async_copy(values, out.at[REACH, 1], local_sem.at[1])
    load_k.start()
    load_v.start()
    load_k.wait()
    load_v.wait()

    def send(source, slot, target, index):
        return pltpu.make_async_remote_copy(
            src_ref=out.at[source],
            dst_ref=out.at[slot],
            send_sem=send_sem.at[index],
            recv_sem=recv_sem.at[slot],
            device_id=place(target),
            device_id_type=MESH,
        )

    send(REACH, 4, me + COLS, 0).start()
    for j in range(3):
        @pl.when(cols[j] > col)
        def _():
            send(REACH, REACH - (cols[j] - col), mates[j], 1 + j).start()
    send(4, 4, me + COLS, 0).wait_recv()
    send(4, 0, me + COLS, 4).start()
    for j in range(3):
        send(4, 4 - (cols[j] - col), mates[j], 5 + j).start()
    send(0, 0, me + COLS, 4).wait_recv()
    for j in range(3):
        @pl.when(cols[j] < col)
        def _():
            send(0, col - cols[j], mates[j], 1 + j).start()
    for slot in (1, 2, 3, 5, 6, 7):
        send(slot, slot, me + COLS, 0).wait_recv()
    for index in range(8):
        send(REACH, 4, me + COLS, index).wait_send()


def gather(keys, values):
    return pl.pallas_call(
        gather_kernel,
        out_shape=jax.ShapeDtypeStruct((REACH + 1, 2, TOK, DH), BF16),
        in_specs=[pl.BlockSpec(memory_space=pl.ANY)] * 2,
        out_specs=pl.BlockSpec(memory_space=pltpu.VMEM),
        scratch_shapes=[
            pltpu.SemaphoreType.DMA((2,)),
            pltpu.SemaphoreType.DMA((8,)),
            pltpu.SemaphoreType.DMA((REACH + 1,)),
        ],
        compiler_params=pltpu.CompilerParams(collective_id=0, has_side_effects=True),
        name="halo_gather",
    )(keys, values)


def nt_dot(a, b):
    return lax.dot_general(a, b, (((1,), (1,)), ((), ())), preferred_element_type=F32)


def dot(a, b):
    return jnp.dot(a, b, preferred_element_type=F32)


def split3(x):
    first = x.astype(BF16)
    rest = x - first.astype(F32)
    second = rest.astype(BF16)
    third = (rest - second.astype(F32)).astype(BF16)
    return first, second, third


def compute_kernel(
    window, live, q_ref, o_ref, g_ref, lse_ref, kv_ref, sk_ref, sv_ref,
    dq_ref, part_ref, own_ref, sink_ref, acc, dq_acc, lse_cols,
):
    head = pl.program_id(0)
    _, _, me = whoami()
    lane = lax.broadcasted_iota(jnp.int32, (TOK, DH), 1)

    @pl.when(head == 0)
    def _():
        acc[...] = jnp.zeros_like(acc)
        sink_ref[...] = jnp.zeros_like(sink_ref)
        pieces = jnp.concatenate(split3(lse_ref[...] * (-1.0 / SCALE)), axis=0)
        row = lax.broadcasted_iota(jnp.int32, (3 * HEADS, DH), 0)
        col = lax.broadcasted_iota(jnp.int32, (3 * HEADS, DH), 1)
        pick = (row == col).astype(BF16)
        lse_cols[...] = lax.dot_general(
            pieces, pick, (((0,), (0,)), ((), ())), preferred_element_type=F32
        )

    q = q_ref[...]
    g = g_ref[...]
    delta = jnp.sum(g.astype(F32) * o_ref[...].astype(F32), axis=1, keepdims=True)
    d1, d2, d3 = split3(-delta)
    minus_delta = jnp.where(
        lane == 0, d1.astype(F32), jnp.where(lane == 1, d2.astype(F32), jnp.where(lane == 2, d3.astype(F32), 0.0))
    ).astype(BF16)
    minus_lse = jnp.where(lane % HEADS == head, lse_cols[...], 0.0).astype(BF16)
    ones = jnp.ones((TOK, DH), BF16)
    q_aug = jnp.concatenate([q, minus_lse], axis=1)
    g_aug = jnp.concatenate([g, minus_delta], axis=1)
    q_t = q.T
    g_t = g.T

    span = window[head]
    s = nt_dot(q_aug, jnp.concatenate([sk_ref[...], ones[:DH]], axis=1))
    p = jnp.where(lane < live[head], jnp.exp2(s * EXP2_SCALE), 0.0)
    ds = p * nt_dot(g_aug, jnp.concatenate([sv_ref[...], ones[:DH]], axis=1))
    ds_low = ds.astype(BF16)
    dq_acc[...] = dot(ds_low, sk_ref[...])
    sink_ref[0] += dot(q_t, ds_low)
    sink_ref[1] += dot(g_t, p.astype(BF16))

    gap = lax.broadcasted_iota(jnp.int32, (TOK, TOK), 0) - lax.broadcasted_iota(jnp.int32, (TOK, TOK), 1)

    def block(back, masked):
        slot = REACH - back
        k = kv_ref[slot, 0]
        v = kv_ref[slot, 1]
        s = nt_dot(q_aug, jnp.concatenate([k, ones], axis=1))
        p = jnp.exp2(s * EXP2_SCALE)
        if masked:
            distance = gap + back * TOK
            p = jnp.where((distance >= 0) & (distance < span), p, 0.0)
        ds = p * nt_dot(g_aug, jnp.concatenate([v, ones], axis=1))
        ds_low = ds.astype(BF16)
        dq_acc[...] += dot(ds_low, k)
        acc[slot, 0] += dot(q_t, ds_low)
        acc[slot, 1] += dot(g_t, p.astype(BF16))

    block(0, True)
    full = jnp.minimum(span // TOK, me + 1)
    count = jnp.minimum((span + TOK - 2) // TOK, me) + 1

    def inner(back, carry):
        block(back, False)
        return carry

    def edge(back, carry):
        block(back, True)
        return carry

    lax.fori_loop(1, full, inner, 0)
    lax.fori_loop(jnp.maximum(full, 1), count, edge, 0)
    dq_ref[...] = dq_acc[...] * SCALE

    @pl.when(head == pl.num_programs(0) - 1)
    def _():
        sink_ref[0] = sink_ref[0] * SCALE
        for slot in range(REACH):
            part_ref[slot, 0] = (acc[slot, 0] * SCALE).astype(BF16)
            part_ref[slot, 1] = acc[slot, 1].astype(BF16)
        own_ref[0] = acc[REACH, 0] * SCALE
        own_ref[1] = acc[REACH, 1]


def compute(queries, outputs, out_grad, lse, key_value, sink_keys, sink_values, window_len, sink_live):
    by_head = pl.BlockSpec((TOK, DH), lambda h: (0, h))

    def whole(shape):
        return pl.BlockSpec(shape, lambda h: (0,) * len(shape))

    smem = pl.BlockSpec(memory_space=pltpu.SMEM)
    return pl.pallas_call(
        compute_kernel,
        grid=(HEADS,),
        out_shape=(
            jax.ShapeDtypeStruct((TOK, HEADS * DH), F32),
            jax.ShapeDtypeStruct((REACH, 2, DH, TOK), BF16),
            jax.ShapeDtypeStruct((2, DH, TOK), F32),
            jax.ShapeDtypeStruct((2, DH, DH), F32),
        ),
        in_specs=[
            smem, smem, by_head, by_head, by_head, whole((HEADS, TOK)),
            whole((REACH + 1, 2, TOK, DH)), whole((DH, DH)), whole((DH, DH)),
        ],
        out_specs=(
            by_head, whole((REACH, 2, DH, TOK)), whole((2, DH, TOK)), whole((2, DH, DH)),
        ),
        scratch_shapes=[
            pltpu.VMEM((REACH + 1, 2, DH, TOK), F32),
            pltpu.VMEM((TOK, DH), F32),
            pltpu.VMEM((TOK, DH), F32),
        ],
        compiler_params=pltpu.CompilerParams(dimension_semantics=("arbitrary",)),
        name="window_backward",
    )(window_len, sink_live, queries, outputs, out_grad, lse, key_value, sink_keys, sink_values)


def reduce_kernel(
    part, own, sink, dk, dv, sk_out, sv_out,
    from_mates, from_far, from_next, from_next_far, sum_near, sum_far, sink_in, sink_mid, sink_buf, sink_sum, sink_all,
    send_sem, recv_sem, s_send, s_recv,
):
    hi, lo, me = whoami()
    col = me % COLS
    mates = [me - col + (col + j) % COLS for j in range(1, COLS)]
    cols = [(col + j) % COLS for j in range(1, COLS)]
    piece = DH * 2 // LO

    barrier = pltpu.get_barrier_semaphore()
    for target in [place(me + COLS), place(me - COLS)]:
        pl.semaphore_signal(barrier, inc=1, device_id=target, device_id_type=MESH)

    def greet_group(i, carry):
        pl.semaphore_signal(barrier, inc=1, device_id=(hi, (lo + i) % LO), device_id_type=MESH)
        pl.semaphore_signal(barrier, inc=1, device_id=((hi + i) % HI, lo), device_id_type=MESH)
        return carry

    lax.fori_loop(1, LO, greet_group, 0)
    pl.semaphore_wait(barrier, 2 + 15 + 15)

    def exchange(phase, source, dest, along_lo):
        def copy(i):
            if along_lo:
                index = (lo + i) % LO
                mine, target = lo, (hi, index)
            else:
                index = (hi + i) % HI
                mine, target = hi, (index, lo)
            return pltpu.make_async_remote_copy(
                src_ref=source(index), dst_ref=dest(mine),
                send_sem=s_send.at[phase, i], recv_sem=s_recv.at[phase, mine],
                device_id=target, device_id_type=MESH,
            )

        def arrival(i):
            base = lo if along_lo else hi
            index = (base + i) % LO
            target = (hi, index) if along_lo else (index, lo)
            return pltpu.make_async_remote_copy(
                src_ref=source(index), dst_ref=dest(index),
                send_sem=s_send.at[phase, i], recv_sem=s_recv.at[phase, index],
                device_id=target, device_id_type=MESH,
            )

        def start():
            def body(i, carry):
                copy(i).start()
                return carry
            lax.fori_loop(1, LO, body, 0)

        def finish():
            def body(i, carry):
                arrival(i).wait_recv()
                copy(i).wait_send()
                return carry
            lax.fori_loop(1, LO, body, 0)

        return start, finish

    start1, finish1 = exchange(0, lambda i: sink.at[i], lambda i: sink_in.at[i], True)
    start2, finish2 = exchange(1, lambda i: sink_sum, lambda i: sink_mid.at[i], False)
    start3, finish3 = exchange(2, lambda i: sink_buf, lambda i: sink_all.at[i], True)

    def send(source, dest, target, index):
        return pltpu.make_async_remote_copy(
            src_ref=source, dst_ref=dest, send_sem=send_sem.at[index], recv_sem=recv_sem.at[index],
            device_id=place(target), device_id_type=MESH,
        )

    def mate_send(j, kind):
        to = 2 - j
        if kind == 0:
            return pltpu.make_async_remote_copy(
                src_ref=part.at[REACH - (4 + col - cols[j])], dst_ref=from_mates.at[to],
                send_sem=send_sem.at[j], recv_sem=recv_sem.at[to],
                device_id=place(mates[j]), device_id_type=MESH,
            )
        back = (col - cols[j] + REACH) % REACH
        return pltpu.make_async_remote_copy(
            src_ref=part.at[REACH - back], dst_ref=from_far.at[to],
            send_sem=send_sem.at[3 + j], recv_sem=recv_sem.at[3 + to],
            device_id=place(mates[j]), device_id_type=MESH,
        )

    def mate_arrival(j, kind):
        dest = from_mates if kind == 0 else from_far
        return pltpu.make_async_remote_copy(
            src_ref=part.at[0], dst_ref=dest.at[j], send_sem=send_sem.at[3 * kind + j],
            recv_sem=recv_sem.at[3 * kind + j], device_id=place(mates[j]), device_id_type=MESH,
        )

    start1()
    for j in range(3):
        mate_send(j, 1).start()
    for j in range(3):
        mate_send(j, 0).start()

    finish1()
    sink_in[lo] = sink[lo]
    total = sink_in[0]
    for i in range(1, LO):
        total = total + sink_in[i]
    sink_sum[...] = total
    start2()

    for j in range(3):
        mate_arrival(j, 1).wait_recv()
    for half in range(2):
        far = part[0, half].astype(F32)
        for j in range(3):
            far = far + jnp.where(cols[j] < col, from_far[j, half].astype(F32), 0.0)
        sum_far[half] = far.astype(BF16)
    far_send = send(sum_far, from_next_far, me - COLS, 6)
    far_send.start()

    finish2()
    sink_mid[hi] = sink_sum[...]
    total = sink_mid[0]
    for i in range(1, HI):
        total = total + sink_mid[i]
    sink_buf[...] = total
    start3()

    for j in range(3):
        mate_arrival(j, 0).wait_recv()
    far_send.wait_recv()
    for half in range(2):
        near = part[REACH - 4, half].astype(F32) + from_next_far[half].astype(F32)
        for j in range(3):
            near = near + from_mates[j, half].astype(F32)
        sum_near[half] = near.astype(BF16)
    near_send = send(sum_near, from_next, me - COLS, 7)
    near_send.start()

    finish3()
    sink_all[lo] = sink_buf[...]
    for i in range(LO // 2):
        sk_out[i * piece:(i + 1) * piece, :] = sink_all[i]
        sv_out[i * piece:(i + 1) * piece, :] = sink_all[LO // 2 + i]

    near_send.wait_recv()
    for half in range(2):
        total = own[half] + from_next[half].astype(F32)
        for j in range(3):
            total = total + jnp.where(cols[j] > col, from_far[j, half].astype(F32), 0.0)
        if half == 0:
            dk[...] = total.T
        else:
            dv[...] = total.T
    for j in range(3):
        mate_send(j, 0).wait_send()
        mate_send(j, 1).wait_send()
    far_send.wait_send()
    near_send.wait_send()


def reduce(part, own, sink):
    piece = DH * 2 // LO
    vmem = pl.BlockSpec(memory_space=pltpu.VMEM)
    block = (2, DH, TOK)
    return pl.pallas_call(
        reduce_kernel,
        out_shape=(
            jax.ShapeDtypeStruct((TOK, DH), F32),
            jax.ShapeDtypeStruct((TOK, DH), F32),
            jax.ShapeDtypeStruct((DH, DH), F32),
            jax.ShapeDtypeStruct((DH, DH), F32),
        ),
        in_specs=[vmem] * 3,
        out_specs=(vmem,) * 4,
        scratch_shapes=[
            pltpu.VMEM((3,) + block, BF16),
            pltpu.VMEM((3,) + block, BF16),
            pltpu.VMEM(block, BF16),
            pltpu.VMEM(block, BF16),
            pltpu.VMEM(block, BF16),
            pltpu.VMEM(block, BF16),
            pltpu.VMEM((LO, piece, DH), F32),
            pltpu.VMEM((HI, piece, DH), F32),
            pltpu.VMEM((piece, DH), F32),
            pltpu.VMEM((piece, DH), F32),
            pltpu.VMEM((LO, piece, DH), F32),
            pltpu.SemaphoreType.DMA((8,)),
            pltpu.SemaphoreType.DMA((8,)),
            pltpu.SemaphoreType.DMA((3, LO)),
            pltpu.SemaphoreType.DMA((3, LO)),
        ],
        compiler_params=pltpu.CompilerParams(collective_id=1, has_side_effects=True),
        name="gradient_reduce",
    )(part, own, sink.reshape(LO, piece, DH))


def on_device(
    queries, keys, values, outputs, out_grad, lse, sink_keys, sink_values, window_len, sink_live
):
    key_value = gather(keys, values)
    query_grad, part, own, sink = compute(
        queries, outputs, out_grad, lse, key_value, sink_keys, sink_values, window_len, sink_live
    )
    key_grad, value_grad, sk_t, sv_t = reduce(part, own, sink)
    return query_grad, key_grad, value_grad, sk_t.T, sv_t.T


def solution(mesh):
    rows = P(("seqhi", "seqlo"), None)
    return jax.shard_map(
        on_device,
        mesh=mesh,
        in_specs=(rows, rows, rows, rows, rows, P(None, ("seqhi", "seqlo")), P(), P(), P(), P()),
        out_specs=(rows, rows, rows, P(), P()),
        check_vma=False,
    )
```

```python
import functools
import math

import jax
import jax.numpy as jnp
from jax import lax
from jax.experimental import pallas as pl
from jax.experimental.pallas import tpu as pltpu
from jax.sharding import PartitionSpec as P

MESH = pl.DeviceIdType.MESH
F32 = jnp.float32
BF16 = jnp.bfloat16
HI = 16
LO = 16
NDEV = HI * LO
COLS = 4
REACH = 8
SINK_SLOT = REACH + 1
TOK = 256
DH = 128
HEADS = 16
SCALE = DH ** (-0.5)
EXP2_SCALE = SCALE * math.log2(math.e)


def place(device):
    device = (device + NDEV) % NDEV
    return (device // LO, device % LO)


def whoami():
    hi, lo = lax.axis_index("seqhi"), lax.axis_index("seqlo")
    return hi, lo, hi * LO + lo


def greet(targets):
    barrier = pltpu.get_barrier_semaphore()
    for target in targets:
        pl.semaphore_signal(barrier, inc=1, device_id=target, device_id_type=MESH)
    pl.semaphore_wait(barrier, len(targets))


def gather_kernel(keys, values, out, local_sem, send_sem, recv_sem):
    _, _, me = whoami()
    col = me % COLS
    mates = [me - col + (col + j) % COLS for j in range(1, COLS)]
    cols = [(col + j) % COLS for j in range(1, COLS)]
    greet([place(me + COLS), place(me - COLS)] + [place(m) for m in mates])

    load_k = pltpu.make_async_copy(keys, out.at[REACH, 0], local_sem.at[0])
    load_v = pltpu.make_async_copy(values, out.at[REACH, 1], local_sem.at[1])
    load_k.start()
    load_v.start()
    load_k.wait()
    load_v.wait()

    def send(source, slot, target, index):
        return pltpu.make_async_remote_copy(
            src_ref=out.at[source],
            dst_ref=out.at[slot],
            send_sem=send_sem.at[index],
            recv_sem=recv_sem.at[slot],
            device_id=place(target),
            device_id_type=MESH,
        )

    send(REACH, 4, me + COLS, 0).start()
    for j in range(3):
        @pl.when(cols[j] > col)
        def _():
            send(REACH, REACH - (cols[j] - col), mates[j], 1 + j).start()
    send(4, 4, me + COLS, 0).wait_recv()
    send(4, 0, me + COLS, 4).start()
    for j in range(3):
        send(4, 4 - (cols[j] - col), mates[j], 5 + j).start()
    send(0, 0, me + COLS, 4).wait_recv()
    for j in range(3):
        @pl.when(cols[j] < col)
        def _():
            send(0, col - cols[j], mates[j], 1 + j).start()
    for slot in (1, 2, 3, 5, 6, 7):
        send(slot, slot, me + COLS, 0).wait_recv()
    for index in range(8):
        send(REACH, 4, me + COLS, index).wait_send()


def gather(keys, values):
    return pl.pallas_call(
        gather_kernel,
        out_shape=jax.ShapeDtypeStruct((REACH + 1, 2, TOK, DH), BF16),
        in_specs=[pl.BlockSpec(memory_space=pl.ANY)] * 2,
        out_specs=pl.BlockSpec(memory_space=pltpu.VMEM),
        scratch_shapes=[
            pltpu.SemaphoreType.DMA((2,)),
            pltpu.SemaphoreType.DMA((8,)),
            pltpu.SemaphoreType.DMA((REACH + 1,)),
        ],
        compiler_params=pltpu.CompilerParams(collective_id=0, has_side_effects=True),
        name="halo_gather",
    )(keys, values)


def nt_dot(a, b):
    return lax.dot_general(a, b, (((1,), (1,)), ((), ())), preferred_element_type=F32)


def dot(a, b):
    return jnp.dot(a, b, preferred_element_type=F32)


def split3(x):
    first = x.astype(BF16)
    rest = x - first.astype(F32)
    second = rest.astype(BF16)
    third = (rest - second.astype(F32)).astype(BF16)
    return first, second, third


def compute_kernel(
    window, live, q_ref, o_ref, g_ref, lse_ref, kv_ref, sk_ref, sv_ref,
    dq_ref, part_ref, own_ref, sink_ref,
    acc, dq_acc, q_aug, g_aug, q_t, g_t, k_aug, v_aug, gaps, lse_cols, ds_buf, p_buf, order, counts,
):
    _, _, me = whoami()
    lane = lax.broadcasted_iota(jnp.int32, (TOK, DH), 1)
    pairs = HEADS // 2

    for i in range(HEADS):
        rank = 0
        for j in range(HEADS):
            if j != i:
                before = window[j] <= window[i] if j < i else window[j] < window[i]
                rank = rank + before.astype(jnp.int32)
        order[rank] = i
    total = pairs
    for i in range(pairs):
        longest = window[order[2 * i + 1]]
        count = jnp.minimum((longest + TOK - 2) // TOK, me) + 1
        counts[i] = count
        total = total + count

    acc[...] = jnp.zeros_like(acc)
    dq_acc[...] = jnp.zeros_like(dq_acc)
    ones = jnp.ones((TOK, DH), BF16)
    for slot in range(REACH + 1):
        k_aug[slot, :, :DH] = kv_ref[slot, 0]
        v_aug[slot, :, :DH] = kv_ref[slot, 1]
        k_aug[slot, :, DH:] = ones
        v_aug[slot, :, DH:] = ones
    zeros = jnp.zeros((TOK, 2 * DH), BF16)
    k_aug[SINK_SLOT] = zeros
    v_aug[SINK_SLOT] = zeros
    k_aug[SINK_SLOT, :DH, :DH] = sk_ref[...]
    v_aug[SINK_SLOT, :DH, :DH] = sv_ref[...]
    k_aug[SINK_SLOT, :DH, DH:] = ones[:DH]
    v_aug[SINK_SLOT, :DH, DH:] = ones[:DH]
    row_at = lax.broadcasted_iota(jnp.int32, (TOK, TOK), 0)
    col_at = lax.broadcasted_iota(jnp.int32, (TOK, TOK), 1)
    gaps[0] = row_at - col_at
    gaps[1] = col_at - row_at
    gaps[2] = col_at

    pieces = jnp.concatenate(split3(lse_ref[...] * (-1.0 / SCALE)), axis=0)
    row = lax.broadcasted_iota(jnp.int32, (3 * HEADS, DH), 0)
    col = lax.broadcasted_iota(jnp.int32, (3 * HEADS, DH), 1)
    pick = (row == col).astype(BF16)
    lse_cols[...] = lax.dot_general(
        pieces, pick, (((0,), (0,)), ((), ())), preferred_element_type=F32
    )

    def prepare(head, carry):
        at = pl.ds(pl.multiple_of(head * DH, DH), DH)
        q = q_ref[:, at]
        g = g_ref[:, at]
        delta = jnp.sum(g.astype(F32) * o_ref[:, at].astype(F32), axis=1, keepdims=True)
        d1, d2, d3 = split3(-delta)
        minus_delta = jnp.where(
            lane == 0, d1.astype(F32),
            jnp.where(lane == 1, d2.astype(F32), jnp.where(lane == 2, d3.astype(F32), 0.0)),
        ).astype(BF16)
        minus_lse = jnp.where(lane % HEADS == head, lse_cols[...], 0.0).astype(BF16)
        q_aug[head, :, :DH] = q
        q_aug[head, :, DH:] = minus_lse
        g_aug[head, :, :DH] = g
        g_aug[head, :, DH:] = minus_delta
        q_t[head] = q.T
        g_t[head] = g.T
        return carry

    lax.fori_loop(0, HEADS, prepare, 0)

    def scores(pair, back, dead):
        sink = back < 0
        slot = jnp.where(sink, SINK_SLOT, REACH - back)
        kind = jnp.where(sink, 2, jnp.where(back == 0, 1, 0))
        first, second = order[2 * pair], order[2 * pair + 1]

        def threshold(head):
            inside = jnp.where(back == 0, 1, window[head] - back * TOK)
            return jnp.where(dead, -(1 << 20), jnp.where(sink, live[head], inside))

        q = jnp.concatenate([q_aug[first], q_aug[second]], axis=0)
        g = jnp.concatenate([g_aug[first], g_aug[second]], axis=0)
        s = nt_dot(q, k_aug[slot])
        dp = nt_dot(g, v_aug[slot])
        p = jnp.exp2(s * EXP2_SCALE)
        gap = gaps[kind]
        inside = jnp.concatenate([gap < threshold(first), gap < threshold(second)], axis=0)
        p = jnp.where(inside, p, 0.0)
        ds_buf[...] = (p * dp).astype(BF16)
        p_buf[...] = p.astype(BF16)

    def gradients(pair, back):
        slot = jnp.where(back < 0, SINK_SLOT, REACH - back)
        first, second = order[2 * pair], order[2 * pair + 1]
        ds = ds_buf[...]
        p = p_buf[...]
        dq = dot(ds, k_aug[slot, :, :DH])
        dk = dot(jnp.concatenate([q_t[first], q_t[second]], axis=1), ds)
        dv = dot(jnp.concatenate([g_t[first], g_t[second]], axis=1), p)
        dq_acc[first] += dq[:TOK]
        dq_acc[second] += dq[TOK:]
        acc[slot, 0] += dk
        acc[slot, 1] += dv

    scores(0, -1, False)

    def step(i, item):
        pair, back = item
        last = back + 1 >= counts[pair]
        next_pair = jnp.minimum(jnp.where(last, pair + 1, pair), pairs - 1)
        next_back = jnp.where(last, -1, back + 1)
        gradients(pair, back)
        scores(next_pair, next_back, i + 1 >= total)
        return next_pair, next_back

    lax.fori_loop(0, total, step, (0, -1))

    for head in range(HEADS):
        dq_ref[:, head * DH:(head + 1) * DH] = dq_acc[head] * SCALE
    sink_ref[0] = acc[SINK_SLOT, 0, :, :DH] * SCALE
    sink_ref[1] = acc[SINK_SLOT, 1, :, :DH]
    for slot in range(REACH):
        part_ref[slot, 0] = (acc[slot, 0] * SCALE).astype(BF16)
        part_ref[slot, 1] = acc[slot, 1].astype(BF16)
    own_ref[0] = acc[REACH, 0] * SCALE
    own_ref[1] = acc[REACH, 1]


def compute(queries, outputs, out_grad, lse, key_value, sink_keys, sink_values, window_len, sink_live):
    smem = pl.BlockSpec(memory_space=pltpu.SMEM)
    vmem = pl.BlockSpec(memory_space=pltpu.VMEM)
    return pl.pallas_call(
        compute_kernel,
        out_shape=(
            jax.ShapeDtypeStruct((TOK, HEADS * DH), F32),
            jax.ShapeDtypeStruct((REACH, 2, DH, TOK), BF16),
            jax.ShapeDtypeStruct((2, DH, TOK), F32),
            jax.ShapeDtypeStruct((2, DH, DH), F32),
        ),
        in_specs=[smem] * 2 + [vmem] * 7,
        out_specs=(vmem,) * 4,
        scratch_shapes=[
            pltpu.VMEM((SINK_SLOT + 1, 2, DH, TOK), F32),
            pltpu.VMEM((HEADS, TOK, DH), F32),
            pltpu.VMEM((HEADS, TOK, 2 * DH), BF16),
            pltpu.VMEM((HEADS, TOK, 2 * DH), BF16),
            pltpu.VMEM((HEADS, DH, TOK), BF16),
            pltpu.VMEM((HEADS, DH, TOK), BF16),
            pltpu.VMEM((SINK_SLOT + 1, TOK, 2 * DH), BF16),
            pltpu.VMEM((SINK_SLOT + 1, TOK, 2 * DH), BF16),
            pltpu.VMEM((3, TOK, TOK), jnp.int32),
            pltpu.VMEM((TOK, DH), F32),
            pltpu.VMEM((2 * TOK, TOK), BF16),
            pltpu.VMEM((2 * TOK, TOK), BF16),
            pltpu.SMEM((HEADS,), jnp.int32),
            pltpu.SMEM((HEADS // 2,), jnp.int32),
        ],
        name="window_backward",
    )(window_len, sink_live, queries, outputs, out_grad, lse, key_value, sink_keys, sink_values)


def reduce_kernel(
    part, own, sink, dk, dv, sk_out, sv_out,
    from_mates, from_far, from_next, from_next_far, sum_near, sum_far, sink_in, sink_mid, sink_buf, sink_sum, sink_all,
    send_sem, recv_sem, s_send, s_recv,
):
    hi, lo, me = whoami()
    col = me % COLS
    mates = [me - col + (col + j) % COLS for j in range(1, COLS)]
    cols = [(col + j) % COLS for j in range(1, COLS)]
    piece = DH * 2 // LO

    barrier = pltpu.get_barrier_semaphore()
    for target in [place(me + COLS), place(me - COLS)]:
        pl.semaphore_signal(barrier, inc=1, device_id=target, device_id_type=MESH)

    def greet_group(i, carry):
        pl.semaphore_signal(barrier, inc=1, device_id=(hi, (lo + i) % LO), device_id_type=MESH)
        pl.semaphore_signal(barrier, inc=1, device_id=((hi + i) % HI, lo), device_id_type=MESH)
        return carry

    lax.fori_loop(1, LO, greet_group, 0)
    pl.semaphore_wait(barrier, 2 + 15 + 15)

    def exchange(phase, source, dest, along_lo):
        def copy(i):
            if along_lo:
                index = (lo + i) % LO
                mine, target = lo, (hi, index)
            else:
                index = (hi + i) % HI
                mine, target = hi, (index, lo)
            return pltpu.make_async_remote_copy(
                src_ref=source(index), dst_ref=dest(mine),
                send_sem=s_send.at[phase, i], recv_sem=s_recv.at[phase, mine],
                device_id=target, device_id_type=MESH,
            )

        def arrival(i):
            base = lo if along_lo else hi
            index = (base + i) % LO
            target = (hi, index) if along_lo else (index, lo)
            return pltpu.make_async_remote_copy(
                src_ref=source(index), dst_ref=dest(index),
                send_sem=s_send.at[phase, i], recv_sem=s_recv.at[phase, index],
                device_id=target, device_id_type=MESH,
            )

        def start():
            def body(i, carry):
                copy(i).start()
                return carry
            lax.fori_loop(1, LO, body, 0)

        def finish():
            def body(i, carry):
                arrival(i).wait_recv()
                copy(i).wait_send()
                return carry
            lax.fori_loop(1, LO, body, 0)

        return start, finish

    start1, finish1 = exchange(0, lambda i: sink.at[i], lambda i: sink_in.at[i], True)
    start2, finish2 = exchange(1, lambda i: sink_sum, lambda i: sink_mid.at[i], False)
    start3, finish3 = exchange(2, lambda i: sink_buf, lambda i: sink_all.at[i], True)

    def send(source, dest, target, index):
        return pltpu.make_async_remote_copy(
            src_ref=source, dst_ref=dest, send_sem=send_sem.at[index], recv_sem=recv_sem.at[index],
            device_id=place(target), device_id_type=MESH,
        )

    def mate_send(j, kind):
        to = 2 - j
        if kind == 0:
            return pltpu.make_async_remote_copy(
                src_ref=part.at[REACH - (4 + col - cols[j])], dst_ref=from_mates.at[to],
                send_sem=send_sem.at[j], recv_sem=recv_sem.at[to],
                device_id=place(mates[j]), device_id_type=MESH,
            )
        back = (col - cols[j] + REACH) % REACH
        return pltpu.make_async_remote_copy(
            src_ref=part.at[REACH - back], dst_ref=from_far.at[to],
            send_sem=send_sem.at[3 + j], recv_sem=recv_sem.at[3 + to],
            device_id=place(mates[j]), device_id_type=MESH,
        )

    def mate_arrival(j, kind):
        dest = from_mates if kind == 0 else from_far
        return pltpu.make_async_remote_copy(
            src_ref=part.at[0], dst_ref=dest.at[j], send_sem=send_sem.at[3 * kind + j],
            recv_sem=recv_sem.at[3 * kind + j], device_id=place(mates[j]), device_id_type=MESH,
        )

    start1()
    for j in range(3):
        mate_send(j, 1).start()
    for j in range(3):
        mate_send(j, 0).start()

    finish1()
    sink_in[lo] = sink[lo]
    total = sink_in[0]
    for i in range(1, LO):
        total = total + sink_in[i]
    sink_sum[...] = total
    start2()

    for j in range(3):
        mate_arrival(j, 1).wait_recv()
    for half in range(2):
        far = part[0, half].astype(F32)
        for j in range(3):
            far = far + jnp.where(cols[j] < col, from_far[j, half].astype(F32), 0.0)
        sum_far[half] = far.astype(BF16)
    far_send = send(sum_far, from_next_far, me - COLS, 6)
    far_send.start()

    finish2()
    sink_mid[hi] = sink_sum[...]
    total = sink_mid[0]
    for i in range(1, HI):
        total = total + sink_mid[i]
    sink_buf[...] = total
    start3()

    for j in range(3):
        mate_arrival(j, 0).wait_recv()
    far_send.wait_recv()
    for half in range(2):
        near = part[REACH - 4, half].astype(F32) + from_next_far[half].astype(F32)
        for j in range(3):
            near = near + from_mates[j, half].astype(F32)
        sum_near[half] = near.astype(BF16)
    near_send = send(sum_near, from_next, me - COLS, 7)
    near_send.start()

    finish3()
    sink_all[lo] = sink_buf[...]
    for i in range(LO // 2):
        sk_out[i * piece:(i + 1) * piece, :] = sink_all[i]
        sv_out[i * piece:(i + 1) * piece, :] = sink_all[LO // 2 + i]

    near_send.wait_recv()
    for half in range(2):
        total = own[half] + from_next[half].astype(F32)
        for j in range(3):
            total = total + jnp.where(cols[j] > col, from_far[j, half].astype(F32), 0.0)
        if half == 0:
            dk[...] = total.T
        else:
            dv[...] = total.T
    for j in range(3):
        mate_send(j, 0).wait_send()
        mate_send(j, 1).wait_send()
    far_send.wait_send()
    near_send.wait_send()


def reduce(part, own, sink):
    piece = DH * 2 // LO
    vmem = pl.BlockSpec(memory_space=pltpu.VMEM)
    block = (2, DH, TOK)
    return pl.pallas_call(
        reduce_kernel,
        out_shape=(
            jax.ShapeDtypeStruct((TOK, DH), F32),
            jax.ShapeDtypeStruct((TOK, DH), F32),
            jax.ShapeDtypeStruct((DH, DH), F32),
            jax.ShapeDtypeStruct((DH, DH), F32),
        ),
        in_specs=[vmem] * 3,
        out_specs=(vmem,) * 4,
        scratch_shapes=[
            pltpu.VMEM((3,) + block, BF16),
            pltpu.VMEM((3,) + block, BF16),
            pltpu.VMEM(block, BF16),
            pltpu.VMEM(block, BF16),
            pltpu.VMEM(block, BF16),
            pltpu.VMEM(block, BF16),
            pltpu.VMEM((LO, piece, DH), F32),
            pltpu.VMEM((HI, piece, DH), F32),
            pltpu.VMEM((piece, DH), F32),
            pltpu.VMEM((piece, DH), F32),
            pltpu.VMEM((LO, piece, DH), F32),
            pltpu.SemaphoreType.DMA((8,)),
            pltpu.SemaphoreType.DMA((8,)),
            pltpu.SemaphoreType.DMA((3, LO)),
            pltpu.SemaphoreType.DMA((3, LO)),
        ],
        compiler_params=pltpu.CompilerParams(collective_id=1, has_side_effects=True),
        name="gradient_reduce",
    )(part, own, sink.reshape(LO, piece, DH))


def on_device(
    queries, keys, values, outputs, out_grad, lse, sink_keys, sink_values, window_len, sink_live
):
    key_value = gather(keys, values)
    query_grad, part, own, sink = compute(
        queries, outputs, out_grad, lse, key_value, sink_keys, sink_values, window_len, sink_live
    )
    key_grad, value_grad, sk_t, sv_t = reduce(part, own, sink)
    return query_grad, key_grad, value_grad, sk_t.T, sv_t.T


def solution(mesh):
    rows = P(("seqhi", "seqlo"), None)
    return jax.shard_map(
        on_device,
        mesh=mesh,
        in_specs=(rows, rows, rows, rows, rows, P(None, ("seqhi", "seqlo")), P(), P(), P(), P()),
        out_specs=(rows, rows, rows, P(), P()),
        check_vma=False,
    )
```

```python
import functools
import math

import jax
import jax.numpy as jnp
from jax import lax
from jax.experimental import pallas as pl
from jax.experimental.pallas import tpu as pltpu
from jax.sharding import PartitionSpec as P

MESH = pl.DeviceIdType.MESH
F32 = jnp.float32
BF16 = jnp.bfloat16
HI = 16
LO = 16
NDEV = HI * LO
COLS = 4
REACH = 8
SINK_SLOT = REACH + 1
TOK = 256
DH = 128
HEADS = 16
SCALE = DH ** (-0.5)
EXP2_SCALE = SCALE * math.log2(math.e)


def place(device):
    device = (device + NDEV) % NDEV
    return (device // LO, device % LO)


def whoami():
    hi, lo = lax.axis_index("seqhi"), lax.axis_index("seqlo")
    return hi, lo, hi * LO + lo


def greet(targets):
    barrier = pltpu.get_barrier_semaphore()
    for target in targets:
        pl.semaphore_signal(barrier, inc=1, device_id=target, device_id_type=MESH)
    pl.semaphore_wait(barrier, len(targets))


def gather_kernel(keys, values, out, local_sem, send_sem, recv_sem):
    _, _, me = whoami()
    col = me % COLS
    mates = [me - col + (col + j) % COLS for j in range(1, COLS)]
    cols = [(col + j) % COLS for j in range(1, COLS)]
    greet([place(me + d) for d in (COLS, -COLS)] + [place(m) for m in mates])

    load_k = pltpu.make_async_copy(keys, out.at[REACH, 0], local_sem.at[0])
    load_v = pltpu.make_async_copy(values, out.at[REACH, 1], local_sem.at[1])
    load_k.start()
    load_v.start()
    load_k.wait()
    load_v.wait()

    def send(source, slot, target, index):
        return pltpu.make_async_remote_copy(
            src_ref=out.at[source],
            dst_ref=out.at[slot],
            send_sem=send_sem.at[index],
            recv_sem=recv_sem.at[slot],
            device_id=place(target),
            device_id_type=MESH,
        )

    send(REACH, 4, me + COLS, 0).start()
    for j in range(3):
        @pl.when(cols[j] > col)
        def _():
            send(REACH, REACH - (cols[j] - col), mates[j], 1 + j).start()
    send(4, 4, me + COLS, 0).wait_recv()
    send(4, 0, me + COLS, 4).start()
    for j in range(3):
        send(4, 4 - (cols[j] - col), mates[j], 5 + j).start()
    send(0, 0, me + COLS, 4).wait_recv()
    for j in range(3):
        @pl.when(cols[j] < col)
        def _():
            send(0, col - cols[j], mates[j], 1 + j).start()
    for slot in (1, 2, 3, 5, 6, 7):
        send(slot, slot, me + COLS, 0).wait_recv()
    for index in range(8):
        send(REACH, 4, me + COLS, index).wait_send()


def gather(keys, values):
    return pl.pallas_call(
        gather_kernel,
        out_shape=jax.ShapeDtypeStruct((REACH + 1, 2, TOK, DH), BF16),
        in_specs=[pl.BlockSpec(memory_space=pl.ANY)] * 2,
        out_specs=pl.BlockSpec(memory_space=pltpu.VMEM),
        scratch_shapes=[
            pltpu.SemaphoreType.DMA((2,)),
            pltpu.SemaphoreType.DMA((8,)),
            pltpu.SemaphoreType.DMA((REACH + 1,)),
        ],
        compiler_params=pltpu.CompilerParams(collective_id=0, has_side_effects=True),
        name="halo_gather",
    )(keys, values)


def nt_dot(a, b):
    return lax.dot_general(a, b, (((1,), (1,)), ((), ())), preferred_element_type=F32)


def dot(a, b):
    return jnp.dot(a, b, preferred_element_type=F32)


def split3(x):
    first = x.astype(BF16)
    rest = x - first.astype(F32)
    second = rest.astype(BF16)
    third = (rest - second.astype(F32)).astype(BF16)
    return first, second, third


def compute_kernel(
    window, live, q_ref, o_ref, g_ref, lse_ref, kv_ref, sk_ref, sv_ref,
    dq_ref, part_ref, own_ref, sink_ref,
    acc, dq_acc, q_aug, g_aug, q_t, g_t, k_aug, v_aug, gaps, lse_cols, ds_a, p_a, ds_b, p_b, order, counts,
):
    _, _, me = whoami()
    lane = lax.broadcasted_iota(jnp.int32, (TOK, DH), 1)
    pairs = HEADS // 2

    for i in range(HEADS):
        rank = 0
        for j in range(HEADS):
            if j != i:
                before = window[j] <= window[i] if j < i else window[j] < window[i]
                rank = rank + before.astype(jnp.int32)
        order[rank] = i
    total = pairs
    for i in range(pairs):
        longest = window[order[2 * i + 1]]
        count = jnp.minimum((longest + TOK - 2) // TOK, me) + 1
        counts[i] = count
        total = total + count

    acc[...] = jnp.zeros_like(acc)
    dq_acc[...] = jnp.zeros_like(dq_acc)
    ones = jnp.ones((TOK, DH), BF16)
    for slot in range(REACH + 1):
        k_aug[slot, :, :DH] = kv_ref[slot, 0]
        v_aug[slot, :, :DH] = kv_ref[slot, 1]
        k_aug[slot, :, DH:] = ones
        v_aug[slot, :, DH:] = ones
    zeros = jnp.zeros((TOK, 2 * DH), BF16)
    k_aug[SINK_SLOT] = zeros
    v_aug[SINK_SLOT] = zeros
    k_aug[SINK_SLOT, :DH, :DH] = sk_ref[...]
    v_aug[SINK_SLOT, :DH, :DH] = sv_ref[...]
    k_aug[SINK_SLOT, :DH, DH:] = ones[:DH]
    v_aug[SINK_SLOT, :DH, DH:] = ones[:DH]
    row_at = lax.broadcasted_iota(jnp.int32, (TOK, TOK), 0)
    col_at = lax.broadcasted_iota(jnp.int32, (TOK, TOK), 1)
    gaps[0] = row_at - col_at
    gaps[1] = col_at - row_at
    gaps[2] = col_at

    pieces = jnp.concatenate(split3(lse_ref[...] * (-1.0 / SCALE)), axis=0)
    row = lax.broadcasted_iota(jnp.int32, (3 * HEADS, DH), 0)
    col = lax.broadcasted_iota(jnp.int32, (3 * HEADS, DH), 1)
    pick = (row == col).astype(BF16)
    lse_cols[...] = lax.dot_general(
        pieces, pick, (((0,), (0,)), ((), ())), preferred_element_type=F32
    )

    def prepare(head, carry):
        at = pl.ds(pl.multiple_of(head * DH, DH), DH)
        q = q_ref[:, at]
        g = g_ref[:, at]
        delta = jnp.sum(g.astype(F32) * o_ref[:, at].astype(F32), axis=1, keepdims=True)
        d1, d2, d3 = split3(-delta)
        minus_delta = jnp.where(
            lane == 0, d1.astype(F32),
            jnp.where(lane == 1, d2.astype(F32), jnp.where(lane == 2, d3.astype(F32), 0.0)),
        ).astype(BF16)
        minus_lse = jnp.where(lane % HEADS == head, lse_cols[...], 0.0).astype(BF16)
        q_aug[head, :, :DH] = q
        q_aug[head, :, DH:] = minus_lse
        g_aug[head, :, :DH] = g
        g_aug[head, :, DH:] = minus_delta
        q_t[head] = q.T
        g_t[head] = g.T
        return carry

    lax.fori_loop(0, HEADS, prepare, 0)

    def scores(item, dead, ds_buf, p_buf):
        pair, back = item
        sink = back < 0
        slot = jnp.where(sink, SINK_SLOT, REACH - back)
        kind = jnp.where(sink, 2, jnp.where(back == 0, 1, 0))
        first, second = order[2 * pair], order[2 * pair + 1]

        def threshold(head):
            inside = jnp.where(back == 0, 1, window[head] - back * TOK)
            return jnp.where(dead, -(1 << 20), jnp.where(sink, live[head], inside))

        q = jnp.concatenate([q_aug[first], q_aug[second]], axis=0)
        g = jnp.concatenate([g_aug[first], g_aug[second]], axis=0)
        s = nt_dot(q, k_aug[slot])
        dp = nt_dot(g, v_aug[slot])
        p = jnp.exp2(s * EXP2_SCALE)
        gap = gaps[kind]
        inside = jnp.concatenate([gap < threshold(first), gap < threshold(second)], axis=0)
        p = jnp.where(inside, p, 0.0)
        ds_buf[...] = (p * dp).astype(BF16)
        p_buf[...] = p.astype(BF16)

    def gradients(item, ds_buf, p_buf):
        pair, back = item
        slot = jnp.where(back < 0, SINK_SLOT, REACH - back)
        first, second = order[2 * pair], order[2 * pair + 1]
        ds = ds_buf[...]
        p = p_buf[...]
        dq = dot(ds, k_aug[slot, :, :DH])
        dk = dot(jnp.concatenate([q_t[first], q_t[second]], axis=1), ds)
        dv = dot(jnp.concatenate([g_t[first], g_t[second]], axis=1), p)
        dq_acc[first] += dq[:TOK]
        dq_acc[second] += dq[TOK:]
        acc[slot, 0] += dk
        acc[slot, 1] += dv

    def advance(item):
        pair, back = item
        last = back + 1 >= counts[pair]
        return jnp.minimum(jnp.where(last, pair + 1, pair), pairs - 1), jnp.where(last, -1, back + 1)

    scores((0, -1), False, ds_a, p_a)

    def step(i, item):
        second = advance(item)
        third = advance(second)
        scores(second, 2 * i + 1 >= total, ds_b, p_b)
        gradients(item, ds_a, p_a)
        scores(third, 2 * i + 2 >= total, ds_a, p_a)
        gradients(second, ds_b, p_b)
        return third

    lax.fori_loop(0, (total + 1) // 2, step, (0, -1))

    for head in range(HEADS):
        dq_ref[:, head * DH:(head + 1) * DH] = dq_acc[head] * SCALE
    sink_ref[0] = acc[SINK_SLOT, 0, :, :DH] * SCALE
    sink_ref[1] = acc[SINK_SLOT, 1, :, :DH]
    for slot in range(REACH):
        part_ref[slot, 0] = (acc[slot, 0] * SCALE).astype(BF16)
        part_ref[slot, 1] = acc[slot, 1].astype(BF16)
    own_ref[0] = acc[REACH, 0] * SCALE
    own_ref[1] = acc[REACH, 1]


def compute(queries, outputs, out_grad, lse, key_value, sink_keys, sink_values, window_len, sink_live):
    smem = pl.BlockSpec(memory_space=pltpu.SMEM)
    vmem = pl.BlockSpec(memory_space=pltpu.VMEM)
    return pl.pallas_call(
        compute_kernel,
        out_shape=(
            jax.ShapeDtypeStruct((TOK, HEADS * DH), F32),
            jax.ShapeDtypeStruct((REACH, 2, DH, TOK), BF16),
            jax.ShapeDtypeStruct((2, DH, TOK), F32),
            jax.ShapeDtypeStruct((2, DH, DH), F32),
        ),
        in_specs=[smem] * 2 + [vmem] * 7,
        out_specs=(vmem,) * 4,
        scratch_shapes=[
            pltpu.VMEM((SINK_SLOT + 1, 2, DH, TOK), F32),
            pltpu.VMEM((HEADS, TOK, DH), F32),
            pltpu.VMEM((HEADS, TOK, 2 * DH), BF16),
            pltpu.VMEM((HEADS, TOK, 2 * DH), BF16),
            pltpu.VMEM((HEADS, DH, TOK), BF16),
            pltpu.VMEM((HEADS, DH, TOK), BF16),
            pltpu.VMEM((SINK_SLOT + 1, TOK, 2 * DH), BF16),
            pltpu.VMEM((SINK_SLOT + 1, TOK, 2 * DH), BF16),
            pltpu.VMEM((3, TOK, TOK), jnp.int32),
            pltpu.VMEM((TOK, DH), F32),
            pltpu.VMEM((2 * TOK, TOK), BF16),
            pltpu.VMEM((2 * TOK, TOK), BF16),
            pltpu.VMEM((2 * TOK, TOK), BF16),
            pltpu.VMEM((2 * TOK, TOK), BF16),
            pltpu.SMEM((HEADS,), jnp.int32),
            pltpu.SMEM((HEADS // 2,), jnp.int32),
        ],
        name="window_backward",
    )(window_len, sink_live, queries, outputs, out_grad, lse, key_value, sink_keys, sink_values)


def reduce_kernel(
    part, own, sink, dk, dv, sk_out, sv_out,
    from_mates, from_far, from_next, from_next_far, sum_near, sum_far, sink_in, sink_mid, sink_buf, sink_sum, sink_all,
    send_sem, recv_sem, s_send, s_recv,
):
    hi, lo, me = whoami()
    col = me % COLS
    mates = [me - col + (col + j) % COLS for j in range(1, COLS)]
    cols = [(col + j) % COLS for j in range(1, COLS)]
    piece = DH * 2 // LO

    barrier = pltpu.get_barrier_semaphore()
    for target in [place(me + d) for d in (COLS, -COLS)]:
        pl.semaphore_signal(barrier, inc=1, device_id=target, device_id_type=MESH)

    def greet_group(i, carry):
        pl.semaphore_signal(barrier, inc=1, device_id=(hi, (lo + i) % LO), device_id_type=MESH)
        pl.semaphore_signal(barrier, inc=1, device_id=((hi + i) % HI, lo), device_id_type=MESH)
        return carry

    lax.fori_loop(1, LO, greet_group, 0)
    pl.semaphore_wait(barrier, 2 + 15 + 15)

    def exchange(phase, source, dest, along_lo):
        def copy(i):
            if along_lo:
                index = (lo + i) % LO
                mine, target = lo, (hi, index)
            else:
                index = (hi + i) % HI
                mine, target = hi, (index, lo)
            return pltpu.make_async_remote_copy(
                src_ref=source(index), dst_ref=dest(mine),
                send_sem=s_send.at[phase, i], recv_sem=s_recv.at[phase, mine],
                device_id=target, device_id_type=MESH,
            )

        def arrival(i):
            base = lo if along_lo else hi
            index = (base + i) % LO
            target = (hi, index) if along_lo else (index, lo)
            return pltpu.make_async_remote_copy(
                src_ref=source(index), dst_ref=dest(index),
                send_sem=s_send.at[phase, i], recv_sem=s_recv.at[phase, index],
                device_id=target, device_id_type=MESH,
            )

        def start():
            def body(i, carry):
                copy(i).start()
                return carry
            lax.fori_loop(1, LO, body, 0)

        def finish():
            def body(i, carry):
                arrival(i).wait_recv()
                copy(i).wait_send()
                return carry
            lax.fori_loop(1, LO, body, 0)

        return start, finish

    start1, finish1 = exchange(0, lambda i: sink.at[i], lambda i: sink_in.at[i], True)
    start2, finish2 = exchange(1, lambda i: sink_sum, lambda i: sink_mid.at[i], False)
    start3, finish3 = exchange(2, lambda i: sink_buf, lambda i: sink_all.at[i], True)

    def send(source, dest, target, index):
        return pltpu.make_async_remote_copy(
            src_ref=source, dst_ref=dest, send_sem=send_sem.at[index], recv_sem=recv_sem.at[index],
            device_id=place(target), device_id_type=MESH,
        )

    def mate_send(j, kind):
        to = 2 - j
        if kind == 0:
            return pltpu.make_async_remote_copy(
                src_ref=part.at[REACH - (4 + col - cols[j])], dst_ref=from_mates.at[to],
                send_sem=send_sem.at[j], recv_sem=recv_sem.at[to],
                device_id=place(mates[j]), device_id_type=MESH,
            )
        back = (col - cols[j] + REACH) % REACH
        return pltpu.make_async_remote_copy(
            src_ref=part.at[REACH - back], dst_ref=from_far.at[to],
            send_sem=send_sem.at[3 + j], recv_sem=recv_sem.at[3 + to],
            device_id=place(mates[j]), device_id_type=MESH,
        )

    def mate_arrival(j, kind):
        dest = from_mates if kind == 0 else from_far
        return pltpu.make_async_remote_copy(
            src_ref=part.at[0], dst_ref=dest.at[j], send_sem=send_sem.at[3 * kind + j],
            recv_sem=recv_sem.at[3 * kind + j], device_id=place(mates[j]), device_id_type=MESH,
        )

    start1()
    for j in range(3):
        mate_send(j, 1).start()
    for j in range(3):
        mate_send(j, 0).start()

    finish1()
    sink_in[lo] = sink[lo]
    total = sink_in[0]
    for i in range(1, LO):
        total = total + sink_in[i]
    sink_sum[...] = total
    start2()

    for j in range(3):
        mate_arrival(j, 1).wait_recv()
    for half in range(2):
        far = part[0, half].astype(F32)
        for j in range(3):
            far = far + jnp.where(cols[j] < col, from_far[j, half].astype(F32), 0.0)
        sum_far[half] = far.astype(BF16)
    far_send = send(sum_far, from_next_far, me - COLS, 6)
    far_send.start()

    finish2()
    sink_mid[hi] = sink_sum[...]
    total = sink_mid[0]
    for i in range(1, HI):
        total = total + sink_mid[i]
    sink_buf[...] = total
    start3()

    for j in range(3):
        mate_arrival(j, 0).wait_recv()
    far_send.wait_recv()
    for half in range(2):
        near = part[REACH - 4, half].astype(F32) + from_next_far[half].astype(F32)
        for j in range(3):
            near = near + from_mates[j, half].astype(F32)
        sum_near[half] = near.astype(BF16)
    near_send = send(sum_near, from_next, me - COLS, 7)
    near_send.start()

    finish3()
    sink_all[lo] = sink_buf[...]
    for i in range(LO // 2):
        sk_out[i * piece:(i + 1) * piece, :] = sink_all[i]
        sv_out[i * piece:(i + 1) * piece, :] = sink_all[LO // 2 + i]

    near_send.wait_recv()
    for half in range(2):
        total = own[half] + from_next[half].astype(F32)
        for j in range(3):
            total = total + jnp.where(cols[j] > col, from_far[j, half].astype(F32), 0.0)
        if half == 0:
            dk[...] = total.T
        else:
            dv[...] = total.T
    for j in range(3):
        mate_send(j, 0).wait_send()
        mate_send(j, 1).wait_send()
    far_send.wait_send()
    near_send.wait_send()


def reduce(part, own, sink):
    piece = DH * 2 // LO
    vmem = pl.BlockSpec(memory_space=pltpu.VMEM)
    block = (2, DH, TOK)
    return pl.pallas_call(
        reduce_kernel,
        out_shape=(
            jax.ShapeDtypeStruct((TOK, DH), F32),
            jax.ShapeDtypeStruct((TOK, DH), F32),
            jax.ShapeDtypeStruct((DH, DH), F32),
            jax.ShapeDtypeStruct((DH, DH), F32),
        ),
        in_specs=[vmem] * 3,
        out_specs=(vmem,) * 4,
        scratch_shapes=[
            pltpu.VMEM((3,) + block, BF16),
            pltpu.VMEM((3,) + block, BF16),
            pltpu.VMEM(block, BF16),
            pltpu.VMEM(block, BF16),
            pltpu.VMEM(block, BF16),
            pltpu.VMEM(block, BF16),
            pltpu.VMEM((LO, piece, DH), F32),
            pltpu.VMEM((HI, piece, DH), F32),
            pltpu.VMEM((piece, DH), F32),
            pltpu.VMEM((piece, DH), F32),
            pltpu.VMEM((LO, piece, DH), F32),
            pltpu.SemaphoreType.DMA((8,)),
            pltpu.SemaphoreType.DMA((8,)),
            pltpu.SemaphoreType.DMA((3, LO)),
            pltpu.SemaphoreType.DMA((3, LO)),
        ],
        compiler_params=pltpu.CompilerParams(collective_id=1, has_side_effects=True),
        name="gradient_reduce",
    )(part, own, sink.reshape(LO, piece, DH))


def finish_kernel(dk, dv, sk_t, sv_t, dk_out, dv_out, sk_out, sv_out):
    dk_out[...] = dk[...]
    dv_out[...] = dv[...]
    sk_out[...] = sk_t[...].T
    sv_out[...] = sv_t[...].T


def finish(dk, dv, sk_t, sv_t):
    vmem = pl.BlockSpec(memory_space=pltpu.VMEM)
    return pl.pallas_call(
        finish_kernel,
        out_shape=[jax.ShapeDtypeStruct(x.shape, F32) for x in (dk, dv, sk_t, sv_t)],
        in_specs=[vmem] * 4,
        out_specs=[vmem] * 4,
        name="finish",
    )(dk, dv, sk_t, sv_t)


def on_device(
    queries, keys, values, outputs, out_grad, lse, sink_keys, sink_values, window_len, sink_live
):
    key_value = gather(keys, values)
    query_grad, part, own, sink = compute(
        queries, outputs, out_grad, lse, key_value, sink_keys, sink_values, window_len, sink_live
    )
    key_grad, value_grad, sk_t, sv_t = reduce(part, own, sink)
    return (query_grad,) + tuple(finish(key_grad, value_grad, sk_t, sv_t))


def solution(mesh):
    rows = P(("seqhi", "seqlo"), None)
    return jax.shard_map(
        on_device,
        mesh=mesh,
        in_specs=(rows, rows, rows, rows, rows, P(None, ("seqhi", "seqlo")), P(), P(), P(), P()),
        out_specs=(rows, rows, rows, P(), P()),
        check_vma=False,
    )
```

```python
import functools
import math

import jax
import jax.numpy as jnp
from jax import lax
from jax.experimental import pallas as pl
from jax.experimental.pallas import tpu as pltpu
from jax.sharding import PartitionSpec as P

MESH = pl.DeviceIdType.MESH
F32 = jnp.float32
BF16 = jnp.bfloat16
HI = 16
LO = 16
NDEV = HI * LO
COLS = 4
REACH = 8
SINK_SLOT = REACH + 1
TOK = 256
DH = 128
HEADS = 16
SCALE = DH ** (-0.5)
EXP2_SCALE = SCALE * math.log2(math.e)


def place(device):
    device = (device + NDEV) % NDEV
    return (device // LO, device % LO)


def whoami():
    hi, lo = lax.axis_index("seqhi"), lax.axis_index("seqlo")
    return hi, lo, hi * LO + lo


def greet(targets):
    barrier = pltpu.get_barrier_semaphore()
    for target in targets:
        pl.semaphore_signal(barrier, inc=1, device_id=target, device_id_type=MESH)
    pl.semaphore_wait(barrier, len(targets))


def nt_dot(a, b):
    return lax.dot_general(a, b, (((1,), (1,)), ((), ())), preferred_element_type=F32)


def dot(a, b):
    return jnp.dot(a, b, preferred_element_type=F32)


def split3(x):
    first = x.astype(BF16)
    rest = x - first.astype(F32)
    second = rest.astype(BF16)
    third = (rest - second.astype(F32)).astype(BF16)
    return first, second, third


def back_of(step, col):
    group, at = (step - 1) // COLS * COLS, (step - 1) % COLS
    back = group + jnp.where(at < col, at + 1, jnp.where(at == col, COLS, at))
    return jnp.where(step > REACH, 0, back)


def fused_kernel(
    window, live, q_hbm, o_hbm, g_hbm, lse_ref, keys, values, sk_ref, sv_ref,
    dq_out, dk, dv, sk_out, sv_out,
    kv, acc, part, dq_acc, q_in, o_in, g_in, q_aug, g_aug, q_t, g_t, gaps, lse_cols, ds_a, p_a, ds_b, p_b,
    from_mates, from_near, from_far, sum_near, sum_far, sink_parts, sink_in, sink_mid, sink_sum, sink_buf, sink_all,
    load_sem, in_send, in_recv, out_send, out_recv, s_send, s_recv,
):
    hi, lo, me = whoami()
    col = me % COLS
    mates = [me - col + (col + j) % COLS for j in range(1, COLS)]
    cols = [(col + j) % COLS for j in range(1, COLS)]
    piece = DH * 2 // LO
    pairs = HEADS // 2

    loads = [
        pltpu.make_async_copy(keys, kv.at[REACH, 0], load_sem.at[0]),
        pltpu.make_async_copy(values, kv.at[REACH, 1], load_sem.at[1]),
        pltpu.make_async_copy(q_hbm, q_in, load_sem.at[2]),
        pltpu.make_async_copy(g_hbm, g_in, load_sem.at[3]),
        pltpu.make_async_copy(o_hbm, o_in, load_sem.at[4]),
    ]
    for copy in loads:
        copy.start()

    barrier = pltpu.get_barrier_semaphore()
    for target in [place(me + d) for d in (COLS, -COLS, REACH, -REACH)]:
        pl.semaphore_signal(barrier, inc=1, device_id=target, device_id_type=MESH)

    def greet_group(i, carry):
        pl.semaphore_signal(barrier, inc=1, device_id=(hi, (lo + i) % LO), device_id_type=MESH)
        pl.semaphore_signal(barrier, inc=1, device_id=((hi + i) % HI, lo), device_id_type=MESH)
        return carry

    lax.fori_loop(1, LO, greet_group, 0)
    pl.semaphore_wait(barrier, 4 + 15 + 15)

    def send_in(source, slot, target, index):
        return pltpu.make_async_remote_copy(
            src_ref=kv.at[source], dst_ref=kv.at[slot],
            send_sem=in_send.at[index], recv_sem=in_recv.at[slot],
            device_id=place(target), device_id_type=MESH,
        )

    loads[0].wait()
    loads[1].wait()
    send_in(REACH, 4, me + COLS, 0).start()
    for j in range(3):
        @pl.when(cols[j] > col)
        def _():
            send_in(REACH, REACH - (cols[j] - col), mates[j], 1 + j).start()

    def pass_near():
        send_in(4, 4, me + COLS, 0).wait_recv()
        send_in(4, 0, me + COLS, 4).start()
        for j in range(3):
            send_in(4, 4 - (cols[j] - col), mates[j], 5 + j).start()

    def pass_far():
        send_in(0, 0, me + COLS, 4).wait_recv()
        for j in range(3):
            @pl.when(cols[j] < col)
            def _():
                send_in(0, col - cols[j], mates[j], 1 + j).start()

    def send_out(back, target):
        near = jnp.where((back > col) & (back <= col + COLS), 0, 1)
        at = back % COLS - 1
        return pltpu.make_async_remote_copy(
            src_ref=part.at[REACH - back], dst_ref=from_mates.at[near, at],
            send_sem=out_send.at[back], recv_sem=out_recv.at[near, at],
            device_id=place(target), device_id_type=MESH,
        )

    def mate_arrival(kind, j):
        return pltpu.make_async_remote_copy(
            src_ref=part.at[0], dst_ref=from_mates.at[kind, j],
            send_sem=out_send.at[1], recv_sem=out_recv.at[kind, j],
            device_id=place(mates[j]), device_id_type=MESH,
        )

    def send_sum(source, dest, target, index):
        return pltpu.make_async_remote_copy(
            src_ref=source, dst_ref=dest, send_sem=out_send.at[index], recv_sem=out_recv.at[index // 4 - 1, 3],
            device_id=place(target), device_id_type=MESH,
        )

    near_send = send_sum(sum_near, from_near, me - COLS, 4)
    far_send = send_sum(sum_far, from_far, me - REACH, 8)

    def flush(step):
        back = back_of(step, col)
        slot = REACH - back

        @pl.when(step <= REACH)
        def _():
            part[slot, 0] = (acc[slot, 0] * SCALE).astype(BF16)
            part[slot, 1] = acc[slot, 1].astype(BF16)

        @pl.when((back != 0) & (back != 4) & (back != 8))
        def _():
            send_out(back, me - col + (col - back + 2 * COLS) % COLS).start()

    def exchange(phase, source, dest, along_lo):
        def copy(i, arriving):
            base = lo if along_lo else hi
            index = (base + i) % LO
            target = (hi, index) if along_lo else (index, lo)
            mine = index if arriving else base
            return pltpu.make_async_remote_copy(
                src_ref=source(index), dst_ref=dest(mine),
                send_sem=s_send.at[phase, i], recv_sem=s_recv.at[phase, mine],
                device_id=target, device_id_type=MESH,
            )

        def start():
            def body(i, carry):
                copy(i, False).start()
                return carry
            lax.fori_loop(1, LO, body, 0)

        def finish():
            def body(i, carry):
                copy(i, True).wait_recv()
                copy(i, False).wait_send()
                return carry
            lax.fori_loop(1, LO, body, 0)

        return start, finish

    start1, finish1 = exchange(0, lambda i: sink_parts.at[i], lambda i: sink_in.at[i], True)
    start2, finish2 = exchange(1, lambda i: sink_sum, lambda i: sink_mid.at[i], False)
    start3, finish3 = exchange(2, lambda i: sink_buf, lambda i: sink_all.at[i], True)

    def sum_of(ref):
        def body(i, total):
            return total + ref[i]
        return lax.fori_loop(1, LO, body, ref[0])

    def sink_begin():
        half = LO // 2
        sink_parts[:half] = (acc[SINK_SLOT, 0, :, :DH] * SCALE).reshape(half, piece, DH)
        sink_parts[half:] = acc[SINK_SLOT, 1, :, :DH].reshape(half, piece, DH)
        start1()

    def sink_second():
        finish1()
        sink_in[lo] = sink_parts[lo]
        sink_sum[...] = sum_of(sink_in)
        start2()

    def sink_third():
        finish2()
        sink_mid[hi] = sink_sum[...]
        sink_buf[...] = sum_of(sink_mid)
        start3()

    acc[...] = jnp.zeros_like(acc)
    dq_acc[...] = jnp.zeros_like(dq_acc)
    kv[SINK_SLOT] = jnp.zeros((2, TOK, DH), BF16)
    kv[SINK_SLOT, 0, :DH] = sk_ref[...]
    kv[SINK_SLOT, 1, :DH] = sv_ref[...]
    row_at = lax.broadcasted_iota(jnp.int32, (TOK, TOK), 0)
    col_at = lax.broadcasted_iota(jnp.int32, (TOK, TOK), 1)
    gaps[0] = row_at - col_at
    gaps[1] = col_at - row_at
    gaps[2] = col_at

    pieces = jnp.concatenate(split3(lse_ref[...] * (-1.0 / SCALE)), axis=0)
    row = lax.broadcasted_iota(jnp.int32, (3 * HEADS, DH), 0)
    column = lax.broadcasted_iota(jnp.int32, (3 * HEADS, DH), 1)
    pick = (row == column).astype(BF16)
    lse_cols[...] = lax.dot_general(
        pieces, pick, (((0,), (0,)), ((), ())), preferred_element_type=F32
    )
    for copy in loads[2:]:
        copy.wait()
    lane = lax.broadcasted_iota(jnp.int32, (TOK, DH), 1)

    def prepare(head, carry):
        at = pl.ds(pl.multiple_of(head * DH, DH), DH)
        q = q_in[:, at]
        g = g_in[:, at]
        delta = jnp.sum(g.astype(F32) * o_in[:, at].astype(F32), axis=1, keepdims=True)
        d1, d2, d3 = split3(-delta)
        minus_delta = jnp.where(
            lane == 0, d1.astype(F32),
            jnp.where(lane == 1, d2.astype(F32), jnp.where(lane == 2, d3.astype(F32), 0.0)),
        ).astype(BF16)
        minus_lse = jnp.where(lane % HEADS == head, lse_cols[...], 0.0).astype(BF16)
        q_aug[head, :, :DH] = q
        q_aug[head, :, DH:] = minus_lse
        g_aug[head, :, :DH] = g
        g_aug[head, :, DH:] = minus_delta
        q_t[head] = q.T
        g_t[head] = g.T
        return carry

    lax.fori_loop(0, HEADS, prepare, 0)
    ones = jnp.ones((TOK, DH), BF16)

    def slot_of(step):
        return jnp.where(step == 0, SINK_SLOT, REACH - back_of(step, col))

    def scores(step, pair, ds_buf, p_buf):
        back = back_of(step, col)
        sink = step == 0
        slot = slot_of(step)
        kind = jnp.where(sink, 2, jnp.where(back == 0, 1, 0))

        def limit(head):
            inside = jnp.where(back == 0, 1, window[head] - back * TOK)
            return jnp.where(sink, live[head], jnp.where(back <= me, inside, -(1 << 20)))

        q = q_aug[pl.ds(2 * pair, 2)].reshape(2 * TOK, 2 * DH)
        g = g_aug[pl.ds(2 * pair, 2)].reshape(2 * TOK, 2 * DH)
        s = nt_dot(q, jnp.concatenate([kv[slot, 0], ones], axis=1))
        dp = nt_dot(g, jnp.concatenate([kv[slot, 1], ones], axis=1))
        p = jnp.exp2(s * EXP2_SCALE)
        gap = gaps[kind]
        inside = jnp.concatenate([gap < limit(2 * pair), gap < limit(2 * pair + 1)], axis=0)
        p = jnp.where(inside, p, 0.0)
        ds_buf[...] = (p * dp).astype(BF16)
        p_buf[...] = p.astype(BF16)

    def gradients(step, pair, ds_buf, p_buf):
        slot = slot_of(step)
        ds = ds_buf[...]
        p = p_buf[...]
        dq = dot(ds, kv[slot, 0])
        dk_t = dot(jnp.concatenate([q_t[2 * pair], q_t[2 * pair + 1]], axis=1), ds)
        dv_t = dot(jnp.concatenate([g_t[2 * pair], g_t[2 * pair + 1]], axis=1), p)
        dq_acc[2 * pair] += dq[:TOK]
        dq_acc[2 * pair + 1] += dq[TOK:]
        acc[slot, 0] += dk_t
        acc[slot, 1] += dv_t

    half_pairs = pairs // 2
    scores(0, 0, ds_a, p_a)

    def body(it, carry):
        step, at = it // half_pairs, it % half_pairs

        @pl.when(at == 0)
        def _():
            @pl.when(step == 1)
            def _():
                sink_begin()

            @pl.when(step == 3)
            def _():
                sink_second()

            @pl.when(step == 5)
            def _():
                sink_third()

            @pl.when(step >= 2)
            def _():
                flush(step - 1)

        @pl.when(at == half_pairs - 1)
        def _():
            @pl.when(step == 0)
            def _():
                pass_near()

            @pl.when(step == 3)
            def _():
                pass_far()

            back = back_of(step + 1, col)

            @pl.when((step + 1 <= REACH) & (back != 4) & (back != 8))
            def _():
                send_in(4, REACH - back, me, 0).wait_recv()

        last = at == half_pairs - 1
        next_step = jnp.minimum(jnp.where(last, step + 1, step), REACH + 1)
        next_pair = jnp.where(last, 0, 2 * at + 2)
        scores(step, 2 * at + 1, ds_b, p_b)
        gradients(step, 2 * at, ds_a, p_a)
        scores(next_step, next_pair, ds_a, p_a)
        gradients(step, 2 * at + 1, ds_b, p_b)
        return carry

    lax.fori_loop(0, (REACH + 2) * half_pairs, body, 0)

    for j in range(3):
        mate_arrival(0, j).wait_recv()
        mate_arrival(1, j).wait_recv()
    for half in range(2):
        total = part[0, half].astype(F32)
        for j in range(3):
            total = total + jnp.where(cols[j] < col, from_mates[1, j, half].astype(F32), 0.0)
        sum_far[half] = total.astype(BF16)
    far_send.start()
    for half in range(2):
        total = part[REACH - 4, half].astype(F32)
        for j in range(3):
            total = total + from_mates[0, j, half].astype(F32)
        sum_near[half] = total.astype(BF16)
    near_send.start()

    for head in range(HEADS):
        dq_out[:, head * DH:(head + 1) * DH] = dq_acc[head] * SCALE

    finish3()
    sink_all[lo] = sink_buf[...]
    for i in range(LO // 2):
        sk_out[i * piece:(i + 1) * piece, :] = sink_all[i]
        sv_out[i * piece:(i + 1) * piece, :] = sink_all[LO // 2 + i]

    near_send.wait_recv()
    far_send.wait_recv()
    for half in range(2):
        total = acc[REACH, half]
        if half == 0:
            total = total * SCALE
        total = total + from_near[half].astype(F32) + from_far[half].astype(F32)
        for j in range(3):
            total = total + jnp.where(cols[j] > col, from_mates[1, j, half].astype(F32), 0.0)
        if half == 0:
            dk[...] = total.T
        else:
            dv[...] = total.T

    for index in range(8):
        send_in(REACH, 4, me + COLS, index).wait_send()
    for back in (1, 2, 3, 5, 6, 7):
        pltpu.make_async_remote_copy(
            src_ref=part.at[REACH - back], dst_ref=from_mates.at[0, 0],
            send_sem=out_send.at[back], recv_sem=out_recv.at[0, 0],
            device_id=place(me + COLS), device_id_type=MESH,
        ).wait_send()
    near_send.wait_send()
    far_send.wait_send()


def fused(queries, outputs, out_grad, lse, keys, values, sink_keys, sink_values, window_len, sink_live):
    smem = pl.BlockSpec(memory_space=pltpu.SMEM)
    vmem = pl.BlockSpec(memory_space=pltpu.VMEM)
    hbm = pl.BlockSpec(memory_space=pl.ANY)
    piece = DH * 2 // LO
    block = (2, DH, TOK)
    wide = (HEADS, TOK, 2 * DH)
    return pl.pallas_call(
        fused_kernel,
        out_shape=(
            jax.ShapeDtypeStruct((TOK, HEADS * DH), F32),
            jax.ShapeDtypeStruct((TOK, DH), F32),
            jax.ShapeDtypeStruct((TOK, DH), F32),
            jax.ShapeDtypeStruct((DH, DH), F32),
            jax.ShapeDtypeStruct((DH, DH), F32),
        ),
        in_specs=[smem] * 2 + [hbm] * 3 + [vmem] + [hbm] * 2 + [vmem] * 2,
        out_specs=(vmem,) * 5,
        scratch_shapes=[
            pltpu.VMEM((SINK_SLOT + 1, 2, TOK, DH), BF16),
            pltpu.VMEM((SINK_SLOT + 1,) + block, F32),
            pltpu.VMEM((REACH,) + block, BF16),
            pltpu.VMEM((HEADS, TOK, DH), F32),
            pltpu.VMEM((TOK, HEADS * DH), BF16),
            pltpu.VMEM((TOK, HEADS * DH), BF16),
            pltpu.VMEM((TOK, HEADS * DH), BF16),
            pltpu.VMEM(wide, BF16),
            pltpu.VMEM(wide, BF16),
            pltpu.VMEM((HEADS, DH, TOK), BF16),
            pltpu.VMEM((HEADS, DH, TOK), BF16),
            pltpu.VMEM((3, TOK, TOK), jnp.int32),
            pltpu.VMEM((TOK, DH), F32),
        ]
        + [pltpu.VMEM((2 * TOK, TOK), BF16)] * 4
        + [pltpu.VMEM((2, 3) + block, BF16)]
        + [pltpu.VMEM(block, BF16)] * 4
        + [
            pltpu.VMEM((LO, piece, DH), F32),
            pltpu.VMEM((LO, piece, DH), F32),
            pltpu.VMEM((HI, piece, DH), F32),
            pltpu.VMEM((piece, DH), F32),
            pltpu.VMEM((piece, DH), F32),
            pltpu.VMEM((LO, piece, DH), F32),
            pltpu.SemaphoreType.DMA((5,)),
            pltpu.SemaphoreType.DMA((8,)),
            pltpu.SemaphoreType.DMA((REACH + 1,)),
            pltpu.SemaphoreType.DMA((REACH + 1,)),
            pltpu.SemaphoreType.DMA((2, 4)),
            pltpu.SemaphoreType.DMA((3, LO)),
            pltpu.SemaphoreType.DMA((3, LO)),
        ],
        compiler_params=pltpu.CompilerParams(collective_id=0, has_side_effects=True),
        name="window_backward",
    )(window_len, sink_live, queries, outputs, out_grad, lse, keys, values, sink_keys, sink_values)


def finish_kernel(dk, dv, sk_t, sv_t, dk_out, dv_out, sk_out, sv_out):
    dk_out[...] = dk[...]
    dv_out[...] = dv[...]
    sk_out[...] = sk_t[...].T
    sv_out[...] = sv_t[...].T


def finish(dk, dv, sk_t, sv_t):
    vmem = pl.BlockSpec(memory_space=pltpu.VMEM)
    return pl.pallas_call(
        finish_kernel,
        out_shape=[jax.ShapeDtypeStruct(x.shape, F32) for x in (dk, dv, sk_t, sv_t)],
        in_specs=[vmem] * 4,
        out_specs=[vmem] * 4,
        name="finish",
    )(dk, dv, sk_t, sv_t)


def on_device(
    queries, keys, values, outputs, out_grad, lse, sink_keys, sink_values, window_len, sink_live
):
    query_grad, key_grad, value_grad, sk_t, sv_t = fused(
        queries, outputs, out_grad, lse, keys, values, sink_keys, sink_values, window_len, sink_live
    )
    return (query_grad,) + tuple(finish(key_grad, value_grad, sk_t, sv_t))


def solution(mesh):
    rows = P(("seqhi", "seqlo"), None)
    return jax.shard_map(
        on_device,
        mesh=mesh,
        in_specs=(rows, rows, rows, rows, rows, P(None, ("seqhi", "seqlo")), P(), P(), P(), P()),
        out_specs=(rows, rows, rows, P(), P()),
        check_vma=False,
    )
```

```python
import functools
import math

import jax
import jax.numpy as jnp
from jax import lax
from jax.experimental import pallas as pl
from jax.experimental.pallas import tpu as pltpu
from jax.sharding import PartitionSpec as P

MESH = pl.DeviceIdType.MESH
F32 = jnp.float32
BF16 = jnp.bfloat16
HI = 16
LO = 16
NDEV = HI * LO
COLS = 4
REACH = 8
SINK_SLOT = REACH + 1
UNROLL = 4
FAR_STEP = 2
TOK = 256
DH = 128
HEADS = 16
SCALE = DH ** (-0.5)
EXP2_SCALE = SCALE * math.log2(math.e)


def place(device):
    device = (device + NDEV) % NDEV
    return (device // LO, device % LO)


def whoami():
    hi, lo = lax.axis_index("seqhi"), lax.axis_index("seqlo")
    return hi, lo, hi * LO + lo


def greet(targets):
    barrier = pltpu.get_barrier_semaphore()
    for target in targets:
        pl.semaphore_signal(barrier, inc=1, device_id=target, device_id_type=MESH)
    pl.semaphore_wait(barrier, len(targets))


def nt_dot(a, b):
    return lax.dot_general(a, b, (((1,), (1,)), ((), ())), preferred_element_type=F32)


def dot(a, b):
    return jnp.dot(a, b, preferred_element_type=F32)


def split3(x):
    first = x.astype(BF16)
    rest = x - first.astype(F32)
    second = rest.astype(BF16)
    third = (rest - second.astype(F32)).astype(BF16)
    return first, second, third


def back_of(step, col):
    group, at = (step - 1) // COLS * COLS, (step - 1) % COLS
    back = group + jnp.where(at < col, at + 1, jnp.where(at == col, COLS, at))
    return jnp.where(step > REACH, 0, back)


def fused_kernel(
    window, live, q_hbm, o_hbm, g_hbm, lse_ref, keys, values, sk_ref, sv_ref,
    dq_out, dk, dv, sk_out, sv_out,
    kv, acc, part, dq_acc, dq_stage, q_in, o_in, g_in, q_heads, g_heads, q_t, g_t, gaps, lse_rep, delta_rep, ds_a, p_a, ds_b, p_b,
    from_mates, from_near, from_far, sum_near, sum_far, sink_parts, sink_in, sink_mid, sink_sum, sink_buf, sink_all,
    load_sem, in_send, in_recv, out_send, out_recv, s_send, s_recv,
):
    hi, lo, me = whoami()
    col = me % COLS
    mates = [me - col + (col + j) % COLS for j in range(1, COLS)]
    cols = [(col + j) % COLS for j in range(1, COLS)]
    piece = DH * 2 // LO
    pairs = HEADS // 2

    loads = [
        pltpu.make_async_copy(keys, kv.at[REACH, 0], load_sem.at[0]),
        pltpu.make_async_copy(values, kv.at[REACH, 1], load_sem.at[1]),
        pltpu.make_async_copy(q_hbm, q_in, load_sem.at[2]),
        pltpu.make_async_copy(g_hbm, g_in, load_sem.at[3]),
        pltpu.make_async_copy(o_hbm, o_in, load_sem.at[4]),
    ]
    for copy in loads:
        copy.start()

    barrier = pltpu.get_barrier_semaphore()
    for target in [place(me + d) for d in (COLS, -COLS, REACH, -REACH)]:
        pl.semaphore_signal(barrier, inc=1, device_id=target, device_id_type=MESH)

    def greet_group(i, carry):
        pl.semaphore_signal(barrier, inc=1, device_id=(hi, (lo + i) % LO), device_id_type=MESH)
        pl.semaphore_signal(barrier, inc=1, device_id=((hi + i) % HI, lo), device_id_type=MESH)
        return carry

    lax.fori_loop(1, LO, greet_group, 0)
    acc[...] = jnp.zeros_like(acc)
    dq_acc[...] = jnp.zeros_like(dq_acc)
    kv[SINK_SLOT] = jnp.zeros((2, TOK, DH), BF16)
    kv[SINK_SLOT, 0, :DH] = sk_ref[...]
    kv[SINK_SLOT, 1, :DH] = sv_ref[...]
    row_at = lax.broadcasted_iota(jnp.int32, (TOK, TOK), 0)
    col_at = lax.broadcasted_iota(jnp.int32, (TOK, TOK), 1)
    gaps[0] = row_at - col_at
    gaps[1] = col_at - row_at
    gaps[2] = col_at

    pl.semaphore_wait(barrier, 4 + 15 + 15)

    def send_in(source, slot, target, index):
        return pltpu.make_async_remote_copy(
            src_ref=kv.at[source], dst_ref=kv.at[slot],
            send_sem=in_send.at[index], recv_sem=in_recv.at[slot],
            device_id=place(target), device_id_type=MESH,
        )

    loads[0].wait()
    loads[1].wait()
    send_in(REACH, 4, me + COLS, 0).start()
    for j in range(3):
        @pl.when(cols[j] > col)
        def _():
            send_in(REACH, REACH - (cols[j] - col), mates[j], 1 + j).start()

    def pass_near():
        send_in(4, 4, me + COLS, 0).wait_recv()
        send_in(4, 0, me + COLS, 4).start()
        for j in range(3):
            send_in(4, 4 - (cols[j] - col), mates[j], 5 + j).start()

    def pass_far():
        send_in(0, 0, me + COLS, 4).wait_recv()
        for j in range(3):
            @pl.when(cols[j] < col)
            def _():
                send_in(0, col - cols[j], mates[j], 1 + j).start()

    def send_out(back, target):
        near = jnp.where((back > col) & (back <= col + COLS), 0, 1)
        at = back % COLS - 1
        return pltpu.make_async_remote_copy(
            src_ref=part.at[REACH - back], dst_ref=from_mates.at[near, at],
            send_sem=out_send.at[back], recv_sem=out_recv.at[near, at],
            device_id=place(target), device_id_type=MESH,
        )

    def mate_arrival(kind, j):
        return pltpu.make_async_remote_copy(
            src_ref=part.at[0], dst_ref=from_mates.at[kind, j],
            send_sem=out_send.at[1], recv_sem=out_recv.at[kind, j],
            device_id=place(mates[j]), device_id_type=MESH,
        )

    def send_sum(source, dest, target, index):
        return pltpu.make_async_remote_copy(
            src_ref=source, dst_ref=dest, send_sem=out_send.at[index], recv_sem=out_recv.at[index // 4 - 1, 3],
            device_id=place(target), device_id_type=MESH,
        )

    near_send = send_sum(sum_near, from_near, me - COLS, 4)
    far_send = send_sum(sum_far, from_far, me - REACH, 8)

    def flush(step):
        back = back_of(step, col)
        slot = REACH - back

        @pl.when(step <= REACH)
        def _():
            part[slot, 0] = (acc[slot, 0] * SCALE).astype(BF16)
            part[slot, 1] = acc[slot, 1].astype(BF16)

        @pl.when((back != 0) & (back != 4) & (back != 8))
        def _():
            send_out(back, me - col + (col - back + 2 * COLS) % COLS).start()

    def exchange(phase, source, dest, along_lo):
        def copy(i, arriving):
            base = lo if along_lo else hi
            index = (base + i) % LO
            target = (hi, index) if along_lo else (index, lo)
            mine = index if arriving else base
            return pltpu.make_async_remote_copy(
                src_ref=source(index), dst_ref=dest(mine),
                send_sem=s_send.at[phase, i], recv_sem=s_recv.at[phase, mine],
                device_id=target, device_id_type=MESH,
            )

        def start():
            def body(i, carry):
                copy(i, False).start()
                return carry
            lax.fori_loop(1, LO, body, 0)

        def finish():
            def body(i, carry):
                copy(i, True).wait_recv()
                copy(i, False).wait_send()
                return carry
            lax.fori_loop(1, LO, body, 0)

        return start, finish

    start1, finish1 = exchange(0, lambda i: sink_parts.at[i], lambda i: sink_in.at[i], True)
    start2, finish2 = exchange(1, lambda i: sink_sum, lambda i: sink_mid.at[i], False)
    start3, finish3 = exchange(2, lambda i: sink_buf, lambda i: sink_all.at[i], True)

    def sum_of(ref):
        def body(i, total):
            return total + ref[i]
        return lax.fori_loop(1, LO, body, ref[0])

    def sink_begin():
        half = LO // 2
        sink_parts[:half] = (acc[SINK_SLOT, 0, :, :DH] * SCALE).reshape(half, piece, DH)
        sink_parts[half:] = acc[SINK_SLOT, 1, :, :DH].reshape(half, piece, DH)
        start1()

    def sink_second():
        finish1()
        sink_in[lo] = sink_parts[lo]
        sink_sum[...] = sum_of(sink_in)
        start2()

    def sink_third():
        finish2()
        sink_mid[hi] = sink_sum[...]
        sink_buf[...] = sum_of(sink_mid)
        start3()

    pieces = jnp.concatenate(split3(lse_ref[...] * math.log2(math.e)), axis=0)
    row = lax.broadcasted_iota(jnp.int32, (3 * HEADS, DH), 0)
    for copy in loads[2:]:
        copy.wait()
    def prepare(head, carry):
        at = pl.ds(pl.multiple_of(head * DH, DH), DH)
        q = q_in[:, at]
        g = g_in[:, at]
        delta = jnp.sum(g.astype(F32) * o_in[:, at].astype(F32), axis=1, keepdims=True)
        delta_rep[head] = jnp.broadcast_to(delta, (TOK, DH))
        pick = (row % HEADS == head).astype(BF16)
        lse_rep[head] = lax.dot_general(
            pieces, pick, (((0,), (0,)), ((), ())), preferred_element_type=F32
        )
        q_heads[head] = q
        g_heads[head] = g
        q_t[head] = q.T
        g_t[head] = g.T
        return carry

    lax.fori_loop(0, HEADS, prepare, 0)

    def slot_of(step):
        return jnp.where(step == 0, SINK_SLOT, REACH - back_of(step, col))

    def twice(x):
        return jnp.concatenate([x, x], axis=1)

    def scores(slot, pair, ds_buf, p_buf):
        back = REACH - slot
        kind = jnp.where(back < 0, 2, jnp.where(back == 0, 1, 0))
        gap = gaps[kind]
        s = nt_dot(q_heads[pl.ds(2 * pair, 2)].reshape(2 * TOK, DH), kv[slot, 0])
        dp = nt_dot(g_heads[pl.ds(2 * pair, 2)].reshape(2 * TOK, DH), kv[slot, 1])
        for u in range(2):
            head = 2 * pair + u
            inside = jnp.where(back == 0, 1, window[head] - back * TOK)
            limit = jnp.where(back < 0, live[head], jnp.where(back <= me, inside, -(1 << 20)))
            at = slice(u * TOK, (u + 1) * TOK)
            p = jnp.exp2(s[at] * EXP2_SCALE - twice(lse_rep[head]))
            p = jnp.where(gap < limit, p, 0.0)
            ds_buf[at] = (p * (dp[at] - twice(delta_rep[head]))).astype(BF16)
            p_buf[at] = p.astype(BF16)

    def gradients(slot, pair, ds_buf, p_buf):
        ds = ds_buf[...]
        p = p_buf[...]
        dq = dot(ds, kv[slot, 0])
        dk_t = dot(jnp.concatenate([q_t[2 * pair], q_t[2 * pair + 1]], axis=1), ds)
        dv_t = dot(jnp.concatenate([g_t[2 * pair], g_t[2 * pair + 1]], axis=1), p)
        dq_acc[2 * pair] += dq[:TOK]
        dq_acc[2 * pair + 1] += dq[TOK:]
        acc[slot, 0] += dk_t
        acc[slot, 1] += dv_t

    turns = pairs // UNROLL
    scores(SINK_SLOT, 0, ds_a, p_a)

    def sum_near_and_send():
        for j in range(3):
            mate_arrival(0, j).wait_recv()
        for half in range(2):
            total = part[REACH - 4, half].astype(F32)
            for j in range(3):
                total = total + from_mates[0, j, half].astype(F32)
            sum_near[half] = total.astype(BF16)
        near_send.start()

    def body(it, carry):
        slot, next_slot = carry
        step, at = it // turns, it % turns

        @pl.when(at == 0)
        def _():
            @pl.when(step == 1)
            def _():
                sink_begin()

            @pl.when(step == 3)
            def _():
                sink_second()

            @pl.when(step == 5)
            def _():
                sink_third()

            @pl.when(step >= 2)
            def _():
                flush(step - 1)

        @pl.when(at == turns - 1)
        def _():
            @pl.when(step == 0)
            def _():
                pass_near()

            @pl.when(step == FAR_STEP)
            def _():
                pass_far()

            @pl.when(step == REACH + 1)
            def _():
                sum_near_and_send()

            back = back_of(step + 1, col)

            @pl.when((step + 1 <= REACH) & (back != 4) & (back != 8))
            def _():
                send_in(4, REACH - back, me, 0).wait_recv()

        last = at == turns - 1
        first = UNROLL * at
        buffers = ((ds_a, p_a), (ds_b, p_b))
        for u in range(UNROLL):
            if u < UNROLL - 1:
                scores(slot, first + u + 1, *buffers[(u + 1) % 2])
            else:
                scores(jnp.where(last, next_slot, slot), jnp.where(last, 0, first + UNROLL), *buffers[0])
            gradients(slot, first + u, *buffers[u % 2])
        return jnp.where(last, next_slot, slot), jnp.where(last, slot_of(jnp.minimum(step + 2, REACH + 1)), next_slot)

    lax.fori_loop(0, (REACH + 2) * turns, body, (jnp.int32(SINK_SLOT), slot_of(1)))

    for j in range(3):
        mate_arrival(1, j).wait_recv()
    for half in range(2):
        total = part[0, half].astype(F32)
        for j in range(3):
            total = total + jnp.where(cols[j] < col, from_mates[1, j, half].astype(F32), 0.0)
        sum_far[half] = total.astype(BF16)
    far_send.start()
    for head in range(HEADS):
        dq_stage[:, head * DH:(head + 1) * DH] = dq_acc[head] * SCALE
    dq_copy = pltpu.make_async_copy(dq_stage, dq_out, load_sem.at[0])
    dq_copy.start()

    finish3()
    sink_all[lo] = sink_buf[...]
    sk_out[...] = sink_all[:LO // 2].reshape(DH, DH).T
    sv_out[...] = sink_all[LO // 2:].reshape(DH, DH).T

    near_send.wait_recv()
    far_send.wait_recv()
    for half in range(2):
        total = acc[REACH, half]
        if half == 0:
            total = total * SCALE
        total = total + from_near[half].astype(F32) + from_far[half].astype(F32)
        for j in range(3):
            total = total + jnp.where(cols[j] > col, from_mates[1, j, half].astype(F32), 0.0)
        if half == 0:
            dk[...] = total.T
        else:
            dv[...] = total.T

    for index in range(8):
        send_in(REACH, 4, me + COLS, index).wait_send()
    for back in (1, 2, 3, 5, 6, 7):
        pltpu.make_async_remote_copy(
            src_ref=part.at[REACH - back], dst_ref=from_mates.at[0, 0],
            send_sem=out_send.at[back], recv_sem=out_recv.at[0, 0],
            device_id=place(me + COLS), device_id_type=MESH,
        ).wait_send()
    near_send.wait_send()
    far_send.wait_send()
    dq_copy.wait()


def fused(queries, outputs, out_grad, lse, keys, values, sink_keys, sink_values, window_len, sink_live):
    smem = pl.BlockSpec(memory_space=pltpu.SMEM)
    vmem = pl.BlockSpec(memory_space=pltpu.VMEM)
    hbm = pl.BlockSpec(memory_space=pltpu.HBM)
    anywhere = pl.BlockSpec(memory_space=pl.ANY)
    piece = DH * 2 // LO
    block = (2, DH, TOK)
    wide = (HEADS, TOK, DH)
    return pl.pallas_call(
        fused_kernel,
        out_shape=(
            jax.ShapeDtypeStruct((TOK, HEADS * DH), F32),
            jax.ShapeDtypeStruct((TOK, DH), F32),
            jax.ShapeDtypeStruct((TOK, DH), F32),
            jax.ShapeDtypeStruct((DH, DH), F32),
            jax.ShapeDtypeStruct((DH, DH), F32),
        ),
        in_specs=[smem] * 2 + [hbm] * 3 + [vmem] + [hbm] * 2 + [vmem] * 2,
        out_specs=(anywhere,) + (vmem,) * 4,
        scratch_shapes=[
            pltpu.VMEM((SINK_SLOT + 1, 2, TOK, DH), BF16),
            pltpu.VMEM((SINK_SLOT + 1,) + block, F32),
            pltpu.VMEM((REACH,) + block, BF16),
            pltpu.VMEM((HEADS, TOK, DH), F32),
            pltpu.VMEM((TOK, HEADS * DH), F32),
            pltpu.VMEM((TOK, HEADS * DH), BF16),
            pltpu.VMEM((TOK, HEADS * DH), BF16),
            pltpu.VMEM((TOK, HEADS * DH), BF16),
            pltpu.VMEM(wide, BF16),
            pltpu.VMEM(wide, BF16),
            pltpu.VMEM((HEADS, DH, TOK), BF16),
            pltpu.VMEM((HEADS, DH, TOK), BF16),
            pltpu.VMEM((3, TOK, TOK), jnp.int32),
            pltpu.VMEM(wide, F32),
            pltpu.VMEM(wide, F32),
        ]
        + [pltpu.VMEM((2 * TOK, TOK), BF16)] * 4
        + [pltpu.VMEM((2, 3) + block, BF16)]
        + [pltpu.VMEM(block, BF16)] * 4
        + [
            pltpu.VMEM((LO, piece, DH), F32),
            pltpu.VMEM((LO, piece, DH), F32),
            pltpu.VMEM((HI, piece, DH), F32),
            pltpu.VMEM((piece, DH), F32),
            pltpu.VMEM((piece, DH), F32),
            pltpu.VMEM((LO, piece, DH), F32),
            pltpu.SemaphoreType.DMA((5,)),
            pltpu.SemaphoreType.DMA((8,)),
            pltpu.SemaphoreType.DMA((REACH + 1,)),
            pltpu.SemaphoreType.DMA((REACH + 1,)),
            pltpu.SemaphoreType.DMA((2, 4)),
            pltpu.SemaphoreType.DMA((3, LO)),
            pltpu.SemaphoreType.DMA((3, LO)),
        ],
        compiler_params=pltpu.CompilerParams(
            collective_id=0, has_side_effects=True, vmem_limit_bytes=36 << 20
        ),
        name="window_backward",
    )(*[
        pltpu.with_memory_space_constraint(x, pltpu.HBM)
        for x in (window_len, sink_live, queries, outputs, out_grad, lse, keys, values, sink_keys, sink_values)
    ])


def finish_kernel(*refs):
    count = len(refs) // 2
    copies = [
        pltpu.make_async_copy(refs[i], refs[count + i], refs[-1].at[i]) for i in range(count)
    ]
    for copy in copies:
        copy.start()
    for copy in copies:
        copy.wait()


def finish(*results):
    anywhere = pl.BlockSpec(memory_space=pl.ANY)
    return pl.pallas_call(
        finish_kernel,
        out_shape=[jax.ShapeDtypeStruct(x.shape, F32) for x in results],
        in_specs=[anywhere] * 5,
        out_specs=[anywhere] * 5,
        scratch_shapes=[pltpu.SemaphoreType.DMA((5,))],
        compiler_params=pltpu.CompilerParams(vmem_limit_bytes=8 << 20),
        name="finish",
    )(*results)


def on_device(
    queries, keys, values, outputs, out_grad, lse, sink_keys, sink_values, window_len, sink_live
):
    return tuple(finish(*fused(
        queries, outputs, out_grad, lse, keys, values, sink_keys, sink_values, window_len, sink_live
    )))


def solution(mesh):
    rows = P(("seqhi", "seqlo"), None)
    return jax.shard_map(
        on_device,
        mesh=mesh,
        in_specs=(rows, rows, rows, rows, rows, P(None, ("seqhi", "seqlo")), P(), P(), P(), P()),
        out_specs=(rows, rows, rows, P(), P()),
        check_vma=False,
    )
```

```python
import functools
import math

import jax
import jax.numpy as jnp
from jax import lax
from jax.experimental import pallas as pl
from jax.experimental.pallas import tpu as pltpu
from jax.sharding import PartitionSpec as P

MESH = pl.DeviceIdType.MESH
F32 = jnp.float32
BF16 = jnp.bfloat16
HI = 16
LO = 16
NDEV = HI * LO
COLS = 4
REACH = 8
SINK_SLOT = REACH + 1
UNROLL = 4
FAR_STEP = 2
EARLY = 10
TOK = 256
DH = 128
HEADS = 16
SCALE = DH ** (-0.5)
EXP2_SCALE = SCALE * math.log2(math.e)


def place(device):
    device = (device + NDEV) % NDEV
    return (device // LO, device % LO)


def whoami():
    hi, lo = lax.axis_index("seqhi"), lax.axis_index("seqlo")
    return hi, lo, hi * LO + lo


def greet(targets):
    barrier = pltpu.get_barrier_semaphore()
    for target in targets:
        pl.semaphore_signal(barrier, inc=1, device_id=target, device_id_type=MESH)
    pl.semaphore_wait(barrier, len(targets))


def nt_dot(a, b):
    return lax.dot_general(a, b, (((1,), (1,)), ((), ())), preferred_element_type=F32)


def dot(a, b):
    return jnp.dot(a, b, preferred_element_type=F32)


def split3(x):
    first = x.astype(BF16)
    rest = x - first.astype(F32)
    second = rest.astype(BF16)
    third = (rest - second.astype(F32)).astype(BF16)
    return first, second, third


def back_of(step, col):
    group, at = (step - 1) // COLS * COLS, (step - 1) % COLS
    back = group + jnp.where(at < col, at + 1, jnp.where(at == col, COLS, at))
    return jnp.where(step > REACH, 0, back)


def fused_kernel(
    window, live, q_hbm, o_hbm, g_hbm, lse_ref, keys, values, sk_ref, sv_ref,
    dq_out, dk, dv, sk_out, sv_out,
    kv, acc, part, dq_acc, dq_stage, q_in, o_in, g_in, q_heads, g_heads, q_t, g_t, gaps, lse_rep, delta_rep, ds_a, p_a, ds_b, p_b,
    from_mates, from_near, from_far, sum_near, sum_far, sink_parts, sink_in, sink_mid, sink_sum, sink_buf, sink_all,
    load_sem, in_send, in_recv, out_send, out_recv, s_send, s_recv,
):
    hi, lo, me = whoami()
    col = me % COLS
    mates = [me - col + (col + j) % COLS for j in range(1, COLS)]
    cols = [(col + j) % COLS for j in range(1, COLS)]
    piece = DH * 2 // LO
    pairs = HEADS // 2

    loads = [
        pltpu.make_async_copy(keys, kv.at[REACH, 0], load_sem.at[0]),
        pltpu.make_async_copy(values, kv.at[REACH, 1], load_sem.at[1]),
        pltpu.make_async_copy(q_hbm, q_in, load_sem.at[2]),
        pltpu.make_async_copy(g_hbm, g_in, load_sem.at[3]),
        pltpu.make_async_copy(o_hbm, o_in, load_sem.at[4]),
    ]
    for copy in loads:
        copy.start()

    barrier = pltpu.get_barrier_semaphore()
    for target in [place(me + d) for d in (COLS, -COLS, REACH, -REACH)]:
        pl.semaphore_signal(barrier, inc=1, device_id=target, device_id_type=MESH)

    def greet_group(i, carry):
        pl.semaphore_signal(barrier, inc=1, device_id=(hi, (lo + i) % LO), device_id_type=MESH)
        pl.semaphore_signal(barrier, inc=1, device_id=((hi + i) % HI, lo), device_id_type=MESH)
        return carry

    lax.fori_loop(1, LO, greet_group, 0)
    acc[...] = jnp.zeros_like(acc)
    dq_acc[...] = jnp.zeros_like(dq_acc)
    kv[SINK_SLOT] = jnp.zeros((2, TOK, DH), BF16)
    kv[SINK_SLOT, 0, :DH] = sk_ref[...]
    kv[SINK_SLOT, 1, :DH] = sv_ref[...]
    row_at = lax.broadcasted_iota(jnp.int32, (TOK, TOK), 0)
    col_at = lax.broadcasted_iota(jnp.int32, (TOK, TOK), 1)
    gaps[0] = row_at - col_at
    gaps[1] = col_at - row_at
    gaps[2] = col_at

    pieces = jnp.concatenate(split3(lse_ref[...] * math.log2(math.e)), axis=0)
    row = lax.broadcasted_iota(jnp.int32, (3 * HEADS, DH), 0)
    for copy in loads[2:]:
        copy.wait()
    def prepare(head, carry):
        at = pl.ds(pl.multiple_of(head * DH, DH), DH)
        q = q_in[:, at]
        g = g_in[:, at]
        delta = jnp.sum(g.astype(F32) * o_in[:, at].astype(F32), axis=1, keepdims=True)
        delta_rep[head] = jnp.broadcast_to(delta, (TOK, DH))
        pick = (row % HEADS == head).astype(BF16)
        lse_rep[head] = lax.dot_general(
            pieces, pick, (((0,), (0,)), ((), ())), preferred_element_type=F32
        )
        q_heads[head] = q
        g_heads[head] = g
        q_t[head] = q.T
        g_t[head] = g.T
        return carry

    lax.fori_loop(0, EARLY, prepare, 0)
    pl.semaphore_wait(barrier, 4 + 15 + 15)

    def send_in(source, slot, target, index):
        return pltpu.make_async_remote_copy(
            src_ref=kv.at[source], dst_ref=kv.at[slot],
            send_sem=in_send.at[index], recv_sem=in_recv.at[slot],
            device_id=place(target), device_id_type=MESH,
        )

    loads[0].wait()
    loads[1].wait()
    send_in(REACH, 4, me + COLS, 0).start()
    for j in range(3):
        @pl.when(cols[j] > col)
        def _():
            send_in(REACH, REACH - (cols[j] - col), mates[j], 1 + j).start()

    def pass_near():
        send_in(4, 4, me + COLS, 0).wait_recv()
        send_in(4, 0, me + COLS, 4).start()
        for j in range(3):
            send_in(4, 4 - (cols[j] - col), mates[j], 5 + j).start()

    def pass_far():
        send_in(0, 0, me + COLS, 4).wait_recv()
        for j in range(3):
            @pl.when(cols[j] < col)
            def _():
                send_in(0, col - cols[j], mates[j], 1 + j).start()

    def send_out(back, target):
        near = jnp.where((back > col) & (back <= col + COLS), 0, 1)
        at = back % COLS - 1
        return pltpu.make_async_remote_copy(
            src_ref=part.at[REACH - back], dst_ref=from_mates.at[near, at],
            send_sem=out_send.at[back], recv_sem=out_recv.at[near, at],
            device_id=place(target), device_id_type=MESH,
        )

    def mate_arrival(kind, j):
        return pltpu.make_async_remote_copy(
            src_ref=part.at[0], dst_ref=from_mates.at[kind, j],
            send_sem=out_send.at[1], recv_sem=out_recv.at[kind, j],
            device_id=place(mates[j]), device_id_type=MESH,
        )

    def send_sum(source, dest, target, index):
        return pltpu.make_async_remote_copy(
            src_ref=source, dst_ref=dest, send_sem=out_send.at[index], recv_sem=out_recv.at[index // 4 - 1, 3],
            device_id=place(target), device_id_type=MESH,
        )

    near_send = send_sum(sum_near, from_near, me - COLS, 4)
    far_send = send_sum(sum_far, from_far, me - REACH, 8)

    def flush(step):
        back = back_of(step, col)
        slot = REACH - back

        @pl.when(step <= REACH)
        def _():
            part[slot, 0] = (acc[slot, 0] * SCALE).astype(BF16)
            part[slot, 1] = acc[slot, 1].astype(BF16)

        @pl.when((back != 0) & (back != 4) & (back != 8))
        def _():
            send_out(back, me - col + (col - back + 2 * COLS) % COLS).start()

    def exchange(phase, source, dest, along_lo):
        def copy(i, arriving):
            base = lo if along_lo else hi
            index = (base + i) % LO
            target = (hi, index) if along_lo else (index, lo)
            mine = index if arriving else base
            return pltpu.make_async_remote_copy(
                src_ref=source(index), dst_ref=dest(mine),
                send_sem=s_send.at[phase, i], recv_sem=s_recv.at[phase, mine],
                device_id=target, device_id_type=MESH,
            )

        def start():
            def body(i, carry):
                copy(i, False).start()
                return carry
            lax.fori_loop(1, LO, body, 0)

        def finish():
            def body(i, carry):
                copy(i, True).wait_recv()
                copy(i, False).wait_send()
                return carry
            lax.fori_loop(1, LO, body, 0)

        return start, finish

    start1, finish1 = exchange(0, lambda i: sink_parts.at[i], lambda i: sink_in.at[i], True)
    start2, finish2 = exchange(1, lambda i: sink_sum, lambda i: sink_mid.at[i], False)
    start3, finish3 = exchange(2, lambda i: sink_buf, lambda i: sink_all.at[i], True)

    def sum_of(ref):
        def body(i, total):
            return total + ref[i]
        return lax.fori_loop(1, LO, body, ref[0])

    def sink_begin():
        half = LO // 2
        sink_parts[:half] = (acc[SINK_SLOT, 0, :, :DH] * SCALE).reshape(half, piece, DH)
        sink_parts[half:] = acc[SINK_SLOT, 1, :, :DH].reshape(half, piece, DH)
        start1()

    def sink_second():
        finish1()
        sink_in[lo] = sink_parts[lo]
        sink_sum[...] = sum_of(sink_in)
        start2()

    def sink_third():
        finish2()
        sink_mid[hi] = sink_sum[...]
        sink_buf[...] = sum_of(sink_mid)
        start3()

    lax.fori_loop(EARLY, HEADS, prepare, 0)

    def slot_of(step):
        return jnp.where(step == 0, SINK_SLOT, REACH - back_of(step, col))

    def twice(x):
        return jnp.concatenate([x, x], axis=1)

    def scores(slot, pair, ds_buf, p_buf):
        back = REACH - slot
        kind = jnp.where(back < 0, 2, jnp.where(back == 0, 1, 0))
        gap = gaps[kind]
        s = nt_dot(q_heads[pl.ds(2 * pair, 2)].reshape(2 * TOK, DH), kv[slot, 0])
        dp = nt_dot(g_heads[pl.ds(2 * pair, 2)].reshape(2 * TOK, DH), kv[slot, 1])
        for u in range(2):
            head = 2 * pair + u
            inside = jnp.where(back == 0, 1, window[head] - back * TOK)
            limit = jnp.where(back < 0, live[head], jnp.where(back <= me, inside, -(1 << 20)))
            at = slice(u * TOK, (u + 1) * TOK)
            p = jnp.exp2(s[at] * EXP2_SCALE - twice(lse_rep[head]))
            p = jnp.where(gap < limit, p, 0.0)
            ds_buf[at] = (p * (dp[at] - twice(delta_rep[head]))).astype(BF16)
            p_buf[at] = p.astype(BF16)

    def gradients(slot, pair, ds_buf, p_buf):
        ds = ds_buf[...]
        p = p_buf[...]
        dq = dot(ds, kv[slot, 0])
        dk_t = dot(jnp.concatenate([q_t[2 * pair], q_t[2 * pair + 1]], axis=1), ds)
        dv_t = dot(jnp.concatenate([g_t[2 * pair], g_t[2 * pair + 1]], axis=1), p)
        dq_acc[2 * pair] += dq[:TOK]
        dq_acc[2 * pair + 1] += dq[TOK:]
        acc[slot, 0] += dk_t
        acc[slot, 1] += dv_t

    turns = pairs // UNROLL
    scores(SINK_SLOT, 0, ds_a, p_a)

    def sum_near_and_send():
        for j in range(3):
            mate_arrival(0, j).wait_recv()
        for half in range(2):
            total = part[REACH - 4, half].astype(F32)
            for j in range(3):
                total = total + from_mates[0, j, half].astype(F32)
            sum_near[half] = total.astype(BF16)
        near_send.start()

    def body(it, carry):
        slot, next_slot = carry
        step, at = it // turns, it % turns

        @pl.when(at == 0)
        def _():
            @pl.when(step == 1)
            def _():
                sink_begin()

            @pl.when(step == 4)
            def _():
                sink_second()

            @pl.when(step == 7)
            def _():
                sink_third()

            @pl.when(step >= 2)
            def _():
                flush(step - 1)

        @pl.when(at == turns - 1)
        def _():
            @pl.when(step == 0)
            def _():
                pass_near()

            @pl.when(step == FAR_STEP)
            def _():
                pass_far()

            @pl.when(step == REACH + 1)
            def _():
                sum_near_and_send()

            back = back_of(step + 1, col)

            @pl.when((step + 1 <= REACH) & (back != 4) & (back != 8))
            def _():
                send_in(4, REACH - back, me, 0).wait_recv()

        last = at == turns - 1
        first = UNROLL * at
        buffers = ((ds_a, p_a), (ds_b, p_b))
        for u in range(UNROLL):
            if u < UNROLL - 1:
                scores(slot, first + u + 1, *buffers[(u + 1) % 2])
            else:
                scores(jnp.where(last, next_slot, slot), jnp.where(last, 0, first + UNROLL), *buffers[0])
            gradients(slot, first + u, *buffers[u % 2])
        return jnp.where(last, next_slot, slot), jnp.where(last, slot_of(jnp.minimum(step + 2, REACH + 1)), next_slot)

    lax.fori_loop(0, (REACH + 2) * turns, body, (jnp.int32(SINK_SLOT), slot_of(1)))

    for j in range(3):
        mate_arrival(1, j).wait_recv()
    for half in range(2):
        total = part[0, half].astype(F32)
        for j in range(3):
            total = total + jnp.where(cols[j] < col, from_mates[1, j, half].astype(F32), 0.0)
        sum_far[half] = total.astype(BF16)
    far_send.start()
    for head in range(HEADS):
        dq_stage[:, head * DH:(head + 1) * DH] = dq_acc[head] * SCALE
    dq_copy = pltpu.make_async_copy(dq_stage, dq_out, load_sem.at[0])
    dq_copy.start()

    finish3()
    sink_all[lo] = sink_buf[...]
    sk_out[...] = sink_all[:LO // 2].reshape(DH, DH).T
    sv_out[...] = sink_all[LO // 2:].reshape(DH, DH).T

    near_send.wait_recv()
    far_send.wait_recv()
    for half in range(2):
        total = acc[REACH, half]
        if half == 0:
            total = total * SCALE
        total = total + from_near[half].astype(F32) + from_far[half].astype(F32)
        for j in range(3):
            total = total + jnp.where(cols[j] > col, from_mates[1, j, half].astype(F32), 0.0)
        if half == 0:
            dk[...] = total.T
        else:
            dv[...] = total.T

    for index in range(8):
        send_in(REACH, 4, me + COLS, index).wait_send()
    for back in (1, 2, 3, 5, 6, 7):
        pltpu.make_async_remote_copy(
            src_ref=part.at[REACH - back], dst_ref=from_mates.at[0, 0],
            send_sem=out_send.at[back], recv_sem=out_recv.at[0, 0],
            device_id=place(me + COLS), device_id_type=MESH,
        ).wait_send()
    near_send.wait_send()
    far_send.wait_send()
    dq_copy.wait()


def fused(queries, outputs, out_grad, lse, keys, values, sink_keys, sink_values, window_len, sink_live):
    smem = pl.BlockSpec(memory_space=pltpu.SMEM)
    vmem = pl.BlockSpec(memory_space=pltpu.VMEM)
    hbm = pl.BlockSpec(memory_space=pltpu.HBM)
    anywhere = pl.BlockSpec(memory_space=pl.ANY)
    piece = DH * 2 // LO
    block = (2, DH, TOK)
    wide = (HEADS, TOK, DH)
    return pl.pallas_call(
        fused_kernel,
        out_shape=(
            jax.ShapeDtypeStruct((TOK, HEADS * DH), F32),
            jax.ShapeDtypeStruct((TOK, DH), F32),
            jax.ShapeDtypeStruct((TOK, DH), F32),
            jax.ShapeDtypeStruct((DH, DH), F32),
            jax.ShapeDtypeStruct((DH, DH), F32),
        ),
        in_specs=[smem] * 2 + [hbm] * 3 + [vmem] + [hbm] * 2 + [vmem] * 2,
        out_specs=(anywhere,) + (vmem,) * 4,
        scratch_shapes=[
            pltpu.VMEM((SINK_SLOT + 1, 2, TOK, DH), BF16),
            pltpu.VMEM((SINK_SLOT + 1,) + block, F32),
            pltpu.VMEM((REACH,) + block, BF16),
            pltpu.VMEM((HEADS, TOK, DH), F32),
            pltpu.VMEM((TOK, HEADS * DH), F32),
            pltpu.VMEM((TOK, HEADS * DH), BF16),
            pltpu.VMEM((TOK, HEADS * DH), BF16),
            pltpu.VMEM((TOK, HEADS * DH), BF16),
            pltpu.VMEM(wide, BF16),
            pltpu.VMEM(wide, BF16),
            pltpu.VMEM((HEADS, DH, TOK), BF16),
            pltpu.VMEM((HEADS, DH, TOK), BF16),
            pltpu.VMEM((3, TOK, TOK), jnp.int32),
            pltpu.VMEM(wide, F32),
            pltpu.VMEM(wide, F32),
        ]
        + [pltpu.VMEM((2 * TOK, TOK), BF16)] * 4
        + [pltpu.VMEM((2, 3) + block, BF16)]
        + [pltpu.VMEM(block, BF16)] * 4
        + [
            pltpu.VMEM((LO, piece, DH), F32),
            pltpu.VMEM((LO, piece, DH), F32),
            pltpu.VMEM((HI, piece, DH), F32),
            pltpu.VMEM((piece, DH), F32),
            pltpu.VMEM((piece, DH), F32),
            pltpu.VMEM((LO, piece, DH), F32),
            pltpu.SemaphoreType.DMA((5,)),
            pltpu.SemaphoreType.DMA((8,)),
            pltpu.SemaphoreType.DMA((REACH + 1,)),
            pltpu.SemaphoreType.DMA((REACH + 1,)),
            pltpu.SemaphoreType.DMA((2, 4)),
            pltpu.SemaphoreType.DMA((3, LO)),
            pltpu.SemaphoreType.DMA((3, LO)),
        ],
        compiler_params=pltpu.CompilerParams(
            collective_id=0, has_side_effects=True, vmem_limit_bytes=36 << 20
        ),
        name="window_backward",
    )(*[
        pltpu.with_memory_space_constraint(x, pltpu.HBM)
        for x in (window_len, sink_live, queries, outputs, out_grad, lse, keys, values, sink_keys, sink_values)
    ])


def finish_kernel(*refs):
    count = len(refs) // 2
    copies = [
        pltpu.make_async_copy(refs[i], refs[count + i], refs[-1].at[i]) for i in range(count)
    ]
    for copy in copies:
        copy.start()
    for copy in copies:
        copy.wait()


def finish(*results):
    anywhere = pl.BlockSpec(memory_space=pl.ANY)
    return pl.pallas_call(
        finish_kernel,
        out_shape=[jax.ShapeDtypeStruct(x.shape, F32) for x in results],
        in_specs=[anywhere] * 5,
        out_specs=[anywhere] * 5,
        scratch_shapes=[pltpu.SemaphoreType.DMA((5,))],
        compiler_params=pltpu.CompilerParams(vmem_limit_bytes=8 << 20),
        name="finish",
    )(*results)


def on_device(
    queries, keys, values, outputs, out_grad, lse, sink_keys, sink_values, window_len, sink_live
):
    return tuple(finish(*fused(
        queries, outputs, out_grad, lse, keys, values, sink_keys, sink_values, window_len, sink_live
    )))


def solution(mesh):
    rows = P(("seqhi", "seqlo"), None)
    return jax.shard_map(
        on_device,
        mesh=mesh,
        in_specs=(rows, rows, rows, rows, rows, P(None, ("seqhi", "seqlo")), P(), P(), P(), P()),
        out_specs=(rows, rows, rows, P(), P()),
        check_vma=False,
    )
```
